256 devices in a mesh: order: 32 (over x, y, core), axial: 8 (over z).
Axes of the slice: x: 4, y: 4, z: 8, core: 2. Of those that a mesh axis runs over, the one named last changes fastest.
Arguments:
- coefficients: bfloat16 [4, 2, 1024, 16, 1024], P(None, None, 'order', 'axial'), may hold values from -0.005859375 to 0.005859375
- order_lists: int32 [1024], replicated, may hold values from 0 to 1023, as said below
- lengths: int32 [1024], replicated, may hold values from 128 to 1024, as said below
Outputs:
- advection: bfloat16 [3, 2, 1024, 16, 1024], P(None, None, 'order', 'axial')
The draws below stay inside these ranges and needn't reach their ends.
Inputs may be any that keep to these rules, and one draw needn't show every extreme that they name: `order_lists`: a permutation of the orders 0 to 1023; the device with index j along order holds slots j * 32 to (j + 1) * 32 - 1 of coefficients and advection. lengths[m] minus (128 + ((1023 - m) * 768) // 1023) lies in 0 to 128.
All inputs are finite; a program needn't handle non-finite values.
Results may differ from the reference program's by a relative error of at most 0.0095.
Values may be sent and summed in bfloat16 or wider, within the bound.
No kernel may reach another device: no remote copies, remote signals or barrier semaphores. Data moves between devices by JAX's collectives and lax.ppermute only.
A program may use at most 128 MiB of HBM per device.

```python
import math
import jax
import jax.numpy as jnp
from jax import lax

M = 1024
R = 1024
K = 1024
NA = 2048
NZ = 16
MO = 32


def draw_order_lists(key, part):
    key_spread, key_blocks, key_shuffle = jax.random.split(jax.random.fold_in(key, 11), 3)
    group_count = M // MO
    position = jnp.arange(M, dtype=jnp.int32)
    spread = jax.random.randint(key_spread, (M,), 0, 4 * MO, dtype=jnp.int32)
    dealt_ids = jnp.argsort((position + spread) * M + position, stable=True).astype(jnp.int32)
    blocks = dealt_ids.reshape(group_count, MO)
    blocks = jnp.take(blocks, jax.random.permutation(key_blocks, group_count), axis=0)
    shuffle = jax.random.randint(key_shuffle, (group_count, MO), 0, M, dtype=jnp.int32)
    inside = jnp.argsort(shuffle * MO + jnp.arange(MO, dtype=jnp.int32)[None, :], axis=1, stable=True)
    blocks = jnp.take_along_axis(blocks, inside, axis=1)
    return blocks.reshape(M).astype(jnp.int32)


def draw_lengths(key, part):
    position = jnp.arange(M, dtype=jnp.int32)
    jitter = jax.random.randint(jax.random.fold_in(key, 23), (M,), 0, K // 8 + 1, dtype=jnp.int32)
    jitter = jnp.where(position == 0, K // 8, jnp.where(position == M - 1, 0, jitter))
    trend = K // 8 + (M - 1 - position) * (K - K // 4) // (M - 1)
    return (trend + jitter).astype(jnp.int32)


def steps_of(key, extent, shards, least, largest):
    def one(dim, parts):
        heights = jax.random.uniform(jax.random.fold_in(jax.random.fold_in(key, 6), dim), (parts,), jnp.float32, least / len(shards), largest / len(shards))
        return jnp.repeat(jnp.exp(heights), extent[dim] // parts).reshape((-1,) + (1,) * (len(extent) - dim - 1))

    loudness = one(*shards[0])
    for cut in shards[1:]:
        loudness = loudness * one(*cut)
    return loudness


def normal_values(key, shape, deviation, bound, cuts=(), kind=jnp.bfloat16):
    drawn = deviation * jax.random.normal(key, shape, jnp.float32)
    if cuts:
        drawn = drawn * steps_of(key, shape, cuts, -0.22, 0.18)
    return jnp.clip(drawn, -bound, bound).astype(kind)


def setup_inputs(seed: int = 0) -> dict:
    key_list = jax.random.split(jax.random.key(seed), 4)
    return {
        "coefficients": normal_values(key_list[0], (4, 2, M, NZ, K), (M * K) ** -0.5, 0.005859375, ((2, 32), (3, 8))),
        "order_lists": draw_order_lists(jax.random.fold_in(key_list[3], 71), 0),
        "lengths": draw_lengths(jax.random.fold_in(key_list[3], 71), 0),
    }


def radial_tables(radius_count, mode_count):
    radius_ids = jnp.arange(radius_count, dtype=jnp.int32)
    mode_ids = jnp.arange(mode_count, dtype=jnp.int32)
    phases = mode_ids[None, :] * (2 * radius_ids[:, None] + 1) % (4 * radius_count)
    angles_rad = phases.astype(jnp.float32) * (math.pi / (2 * radius_count))
    synthesis = jnp.cos(angles_rad).astype(jnp.bfloat16)
    analysis = (jnp.cos(angles_rad.T) * math.sqrt(2.0 / radius_count)).astype(jnp.bfloat16)
    return (synthesis, analysis)

def azimuthal_tables(order_ids, point_count):
    points = jnp.arange(point_count, dtype=jnp.int32)
    phases = order_ids[..., None] * points % point_count
    angles_rad = phases.astype(jnp.float32) * (2.0 * math.pi / point_count)
    cosines = jnp.cos(angles_rad)
    sines = jnp.sin(angles_rad)
    weight = jnp.where(order_ids == 0, 1.0, 2.0).astype(jnp.float32)[..., None]
    forward = jnp.stack((weight * cosines, -weight * sines), axis=-3).astype(jnp.bfloat16)
    factor = math.sqrt(2.0 / point_count)
    inverse = jnp.stack((cosines * factor, -sines * factor), axis=-3).astype(jnp.bfloat16)
    return (forward, inverse)

def reference(coefficients, order_lists, lengths):
    synthesis, analysis = radial_tables(R, K)
    forward, inverse = azimuthal_tables(order_lists, NA)
    synthesis_f = synthesis.astype(jnp.float32)
    analysis_f = analysis.astype(jnp.float32)
    forward_f = forward.astype(jnp.float32)
    inverse_f = inverse.astype(jnp.float32)
    slot_lengths = jnp.take(lengths, order_lists.astype(jnp.int32))
    retained = jnp.arange(K, dtype=jnp.int32)[None, :] < slot_lengths[:, None]
    plane_major = jnp.moveaxis(coefficients, 3, 0)

    def to_physical(plane_in):
        masked = jnp.where(retained[None, None], plane_in, 0).astype(jnp.float32)
        radial = jnp.einsum('fcmk,rk->fcmr', masked, synthesis_f).astype(jnp.bfloat16)
        physical = jnp.einsum('fcmr,cmj->frj', radial.astype(jnp.float32), forward_f)
        return physical.astype(jnp.bfloat16)
    physical = lax.map(to_physical, plane_major)
    plane_total = physical.shape[0]

    def advect(position):

        def plane_at(offset):
            where_at = ((position + offset) % plane_total).astype(jnp.int32)
            return lax.dynamic_index_in_dim(physical, where_at, 0, keepdims=False).astype(jnp.float32)
        current = plane_at(0)
        ahead_one = plane_at(1)
        behind_one = plane_at(-1)
        ahead_two = plane_at(2)
        behind_two = plane_at(-2)
        gradient = (8.0 * (ahead_one[:3] - behind_one[:3]) - (ahead_two[:3] - behind_two[:3])) / 12.0
        products = (current[3][None] * gradient).astype(jnp.bfloat16)
        spectral = jnp.einsum('grj,cmj->gcmr', products.astype(jnp.float32), inverse_f).astype(jnp.bfloat16)
        result = jnp.einsum('gcmr,kr->gcmk', spectral.astype(jnp.float32), analysis_f)
        return jnp.where(retained[None, None], result, 0.0).astype(jnp.bfloat16)
    advected = lax.map(advect, jnp.arange(plane_total, dtype=jnp.int32))
    return jnp.moveaxis(advected, 0, 3)
```

```python
import functools
import math

import jax
import jax.numpy as jnp
import numpy as np
from jax import lax
from jax.experimental import pallas as pl
from jax.experimental.pallas import tpu as pltpu
from jax.sharding import PartitionSpec as P

R = 1024
F32 = jnp.float32
BF16 = jnp.bfloat16


def radial_constants(radius_count, mode_count):
    radius_ids = np.arange(radius_count)
    mode_ids = np.arange(mode_count)
    phases = mode_ids[None, :] * (2 * radius_ids[:, None] + 1) % (4 * radius_count)
    cosines = np.cos(phases * (math.pi / (2 * radius_count))).astype(np.float32)
    synthesis = cosines.astype(jnp.bfloat16)
    analysis = (cosines * np.float32(math.sqrt(2.0 / radius_count))).astype(jnp.bfloat16)
    return synthesis, analysis


def plane_matrices(slots):
    width = 2 * slots * 2
    pair = width // 2
    inner = np.arange(width)
    plane, rest = inner % 2, inner // 2
    gather = np.zeros((width, width), np.float32)
    gather[inner, plane * pair + rest] = 1.0
    eye = np.eye(pair, dtype=np.float32)
    own = np.kron(eye, np.array([[0, 8], [-8, 0]], np.float32))
    low = np.kron(eye, np.array([[1, -8], [0, 1]], np.float32))
    high = np.kron(eye, np.array([[-1, 0], [8, -1]], np.float32))
    rows = np.concatenate([own, low, high], axis=1)
    swap = np.roll(np.eye(width, dtype=np.float32), pair, axis=1)
    both = np.concatenate([gather, gather @ swap], axis=1)
    slope = rows.T @ both
    return (
        rows.astype(jnp.bfloat16),
        both.astype(jnp.bfloat16),
        slope.astype(jnp.bfloat16),
        gather.T.astype(jnp.bfloat16),
    )


def dot(a, b, dims):
    return lax.dot_general(a, b, (dims, ((), ())), preferred_element_type=F32)


def masked_rows(block, lens, weight):
    modes = lax.broadcasted_iota(jnp.int32, block.shape, 1)
    return jnp.where(modes < lens, block.astype(F32) * weight, 0.0)


def raw_kernel(x_ref, lens_ref, weight_ref, table_ref, out_ref, held):
    @pl.when(pl.program_id(0) == 0)
    def _():
        for start in range(0, x_ref.shape[0], 128):
            part = pl.ds(start, 128)
            held[part, :] = masked_rows(x_ref[part, :], lens_ref[...], weight_ref[...]).astype(BF16)

    out_ref[...] = dot(table_ref[...], held[...], ((1,), (1,))).astype(BF16)


def slope_kernel(x_ref, low_ref, high_ref, lens_ref, weight_ref, rows_ref, table_ref, out_ref, held):
    @pl.when(pl.program_id(0) == 0)
    def _():
        for start in range(0, x_ref.shape[0], 128):
            part = pl.ds(start, 128)
            stacked = jnp.concatenate([x_ref[part, :], low_ref[part, :], high_ref[part, :]], axis=0)
            slope = dot(rows_ref[...], stacked, ((1,), (0,)))
            held[part, :] = masked_rows(slope, lens_ref[...], weight_ref[...]).astype(BF16)

    out_ref[...] = dot(table_ref[...], held[...], ((1,), (1,))).astype(BF16)


def whole(shape):
    return pl.BlockSpec(shape, lambda i: (0,) * len(shape))


def radial_raw(x, lens, weight, table, step=256):
    rows, modes = x.shape
    return pl.pallas_call(
        raw_kernel,
        grid=(R // step,),
        out_shape=jax.ShapeDtypeStruct((R, rows), BF16),
        in_specs=[whole(x.shape), whole(lens.shape), whole(weight.shape),
                  pl.BlockSpec((step, modes), lambda i: (i, 0))],
        out_specs=pl.BlockSpec((step, rows), lambda i: (i, 0)),
        scratch_shapes=[pltpu.VMEM((rows, modes), BF16)],
        compiler_params=pltpu.CompilerParams(vmem_limit_bytes=24 << 20),
        name="radial_raw",
    )(x, lens, weight, table)


def radial_slope(x, low, high, lens, weight, rows_map, table, step=256):
    rows, modes = x.shape
    return pl.pallas_call(
        slope_kernel,
        grid=(R // step,),
        out_shape=jax.ShapeDtypeStruct((R, rows), BF16),
        in_specs=[whole(x.shape), whole(x.shape), whole(x.shape), whole(lens.shape),
                  whole(weight.shape), whole(rows_map.shape),
                  pl.BlockSpec((step, modes), lambda i: (i, 0))],
        out_specs=pl.BlockSpec((step, rows), lambda i: (i, 0)),
        scratch_shapes=[pltpu.VMEM((rows, modes), BF16)],
        compiler_params=pltpu.CompilerParams(vmem_limit_bytes=24 << 20),
        name="radial_slope",
    )(x, low, high, lens, weight, rows_map, table)


def table_kernel(orders_ref, out_ref):
    slots = orders_ref.shape[0]
    points = out_ref.shape[1]
    orders = jnp.broadcast_to(orders_ref[...], (slots, 128))
    lane = lax.broadcasted_iota(jnp.int32, (slots, 128), 1)
    unit = 2.0 * math.pi / points
    fine = ((orders * lane) & (points - 1)).astype(F32) * unit
    turn = ((orders * 128) & (points - 1)).astype(F32) * unit
    cos_now, sin_now = jnp.cos(fine), jnp.sin(fine)
    cos_turn, sin_turn = jnp.cos(turn), jnp.sin(turn)
    for block in range(points // 128):
        part = pl.ds(block * 128, 128)
        out_ref[0:slots, part] = cos_now.astype(BF16)
        out_ref[slots:2 * slots, part] = (-sin_now).astype(BF16)
        cos_now, sin_now = (
            cos_now * cos_turn - sin_now * sin_turn,
            sin_now * cos_turn + cos_now * sin_turn,
        )


def azimuthal_table(orders, groups, slots, points):
    return pl.pallas_call(
        table_kernel,
        grid=(groups,),
        out_shape=jax.ShapeDtypeStruct((groups * 2 * slots, points), BF16),
        in_specs=[pl.BlockSpec((slots, 1), lambda i: (i, 0))],
        out_specs=pl.BlockSpec((2 * slots, points), lambda i: (i, 0)),
        compiler_params=pltpu.CompilerParams(vmem_limit_bytes=24 << 20),
        name="azimuthal_table",
    )(orders)


def physical_kernel(groups, band, scale, raw_ref, slope_ref, low_ref, high_ref, both_ref,
                    dz_ref, table_ref, out_ref, lhs, acc):
    step = pl.program_id(0)
    width = both_ref.shape[0]
    half = width // 2
    low_lanes = lax.broadcasted_iota(jnp.int32, (band, width), 1) < half

    @pl.when(step == 0)
    def _():
        acc[...] = jnp.zeros_like(acc)
        for field in range(4):
            if field < 2:
                mapped = dot(slope_ref[:, field * width:(field + 1) * width], both_ref[...], ((1,), (0,)))
            elif field == 2:
                joined = jnp.concatenate([raw_ref[:, 0:width], low_ref[...], high_ref[...]], axis=1)
                mapped = dot(joined, dz_ref[...], ((1,), (0,)))
            else:
                mapped = dot(raw_ref[:, width:2 * width], both_ref[...], ((1,), (0,)))
            for pair in range(groups // 2):
                even = mapped[2 * pair * band:(2 * pair + 1) * band]
                odd = mapped[(2 * pair + 1) * band:(2 * pair + 2) * band]
                first = jnp.where(low_lanes, even[:, :width], odd[:, width:])
                second = jnp.where(low_lanes, even[:, width:], odd[:, :width])
                cols = pl.ds(pair * width, width)
                lhs[(2 * field) * band:(2 * field + 1) * band, cols] = first.astype(BF16)
                lhs[(2 * field + 1) * band:(2 * field + 2) * band, cols] = second.astype(BF16)

    values = dot(lhs[...], table_ref[...], ((1,), (0,)))
    axial = values[6 * band:8 * band] * (1.0 / 12.0)
    products = jnp.concatenate(
        [(values[2 * g * band:(2 * g + 2) * band] * axial).astype(BF16) for g in range(3)], axis=0
    )
    acc[...] += dot(products, table_ref[...], ((1,), (1,)))

    @pl.when(step == pl.num_programs(0) - 1)
    def _():
        for g in range(3):
            for pair in range(groups // 2):
                cols = pl.ds(pair * width, width)
                first = acc[(2 * g) * band:(2 * g + 1) * band, cols] * scale
                second = acc[(2 * g + 1) * band:(2 * g + 2) * band, cols] * scale
                even = jnp.where(low_lanes, first, pltpu.roll(second, half, 1))
                odd = jnp.where(low_lanes, pltpu.roll(first, half, 1), second)
                out_cols = pl.ds(g * width, width)
                out_ref[2 * pair * band:(2 * pair + 1) * band, out_cols] = even.astype(BF16)
                out_ref[(2 * pair + 1) * band:(2 * pair + 2) * band, out_cols] = odd.astype(BF16)


def physical_stage(raw, slope, low, high, both, dz, table, groups, band, step=512):
    rows, points = table.shape
    width = both.shape[0]
    return pl.pallas_call(
        functools.partial(physical_kernel, groups, band, math.sqrt(2.0 / points)),
        grid=(points // step,),
        out_shape=jax.ShapeDtypeStruct((groups * band, 3 * width), BF16),
        in_specs=[whole(raw.shape), whole(slope.shape), whole(low.shape), whole(high.shape),
                  whole(both.shape), whole(dz.shape),
                  pl.BlockSpec((rows, step), lambda i: (0, i))],
        out_specs=whole((groups * band, 3 * width)),
        scratch_shapes=[pltpu.VMEM((8 * band, rows), BF16), pltpu.VMEM((6 * band, rows), F32)],
        compiler_params=pltpu.CompilerParams(vmem_limit_bytes=40 << 20),
        name="physical_stage",
    )(raw, slope, low, high, both, dz, table)


def final_kernel(x_ref, lens_ref, back_ref, table_ref, out_ref, held):
    width = back_ref.shape[0]
    step = pl.program_id(0)
    columns = table_ref.shape[1]

    @pl.when(step == 0)
    def _():
        for g in range(3):
            part = slice(g * width, (g + 1) * width)
            held[:, part] = dot(x_ref[:, part], back_ref[...], ((1,), (0,))).astype(BF16)

    result = dot(held[...], table_ref[...], ((0,), (0,)))
    modes = lax.broadcasted_iota(jnp.int32, (width, columns), 1) + step * columns
    keep = modes < lens_ref[...]
    for g in range(3):
        out_ref[g * width:(g + 1) * width, :] = jnp.where(
            keep, result[g * width:(g + 1) * width], 0.0
        ).astype(BF16)


def radial_analysis(x, lens, back, table, step=256):
    radii, lanes = x.shape
    modes = table.shape[1]
    return pl.pallas_call(
        final_kernel,
        grid=(modes // step,),
        out_shape=jax.ShapeDtypeStruct((lanes, modes), BF16),
        in_specs=[whole(x.shape), whole(lens.shape), whole(back.shape),
                  pl.BlockSpec((radii, step), lambda i: (0, i))],
        out_specs=pl.BlockSpec((lanes, step), lambda i: (0, i)),
        scratch_shapes=[pltpu.VMEM((radii, lanes), BF16)],
        compiler_params=pltpu.CompilerParams(vmem_limit_bytes=24 << 20),
        name="radial_analysis",
    )(x, lens, back, table)


def shift(block, offset):
    count = lax.axis_size("axial")
    return lax.ppermute(block, "axial", [(i, (i + offset) % count) for i in range(count)])


def exchange(block):
    return lax.all_to_all(block, "order", split_axis=0, concat_axis=0, tiled=True)


def shards(coefficients, order_lists, lengths):
    field_count, part_count, slots, planes, modes = coefficients.shape
    order_count = order_lists.shape[0]
    points = 2 * order_count
    groups = lax.axis_size("order")
    band = R // groups
    width = part_count * slots * planes
    synthesis, analysis = radial_constants(R, modes)
    rows_map, both, dz, back = plane_matrices(slots)

    rows = coefficients.reshape(field_count * width, modes)
    sloped, raw = rows[:2 * width], rows[2 * width:]
    low, high = shift(sloped, 1), shift(sloped, -1)

    owned = lax.dynamic_slice_in_dim(order_lists, lax.axis_index("order") * slots, slots)
    catalog = jnp.arange(order_count, dtype=jnp.int32)
    own_lengths = jnp.sum(
        jnp.where(owned[:, None] == catalog[None, :], lengths[None, :], 0), axis=1
    )
    spread = (part_count, slots, planes)
    lens = jnp.broadcast_to(own_lengths[None, :, None], spread).reshape(width, 1)
    weight = jnp.where(owned == 0, 1.0, 2.0).astype(F32)
    weight = jnp.broadcast_to(weight[None, :, None], spread).reshape(width, 1)

    raw_bands = exchange(radial_raw(raw, lens, weight, synthesis))
    table = azimuthal_table(order_lists.reshape(order_count, 1), groups, slots, points)
    own_band = raw_bands[:, :width]
    low_band, high_band = shift(own_band, 1), shift(own_band, -1)
    slope_bands = exchange(radial_slope(sloped, low, high, lens, weight, rows_map, synthesis))
    spectral = physical_stage(
        raw_bands, slope_bands, low_band, high_band, both, dz, table, groups, band
    )
    result = radial_analysis(exchange(spectral), lens, back, analysis)
    return result.reshape(3, part_count, slots, planes, modes)


def solution(mesh):
    placed = (P(None, None, "order", "axial", None), P(), P())
    return jax.shard_map(
        shards,
        mesh=mesh,
        in_specs=placed,
        out_specs=P(None, None, "order", "axial", None),
        check_vma=False,
    )
```

```python
import functools
import math

import jax
import jax.numpy as jnp
import numpy as np
from jax import lax
from jax.experimental import pallas as pl
from jax.experimental.pallas import tpu as pltpu
from jax.sharding import PartitionSpec as P

R = 1024
F32 = jnp.float32
BF16 = jnp.bfloat16


def radial_constants(radius_count, mode_count):
    radius_ids = np.arange(radius_count)
    mode_ids = np.arange(mode_count)
    phases = mode_ids[None, :] * (2 * radius_ids[:, None] + 1) % (4 * radius_count)
    cosines = np.cos(phases * (math.pi / (2 * radius_count))).astype(np.float32)
    synthesis = cosines.astype(jnp.bfloat16)
    analysis = (cosines * np.float32(math.sqrt(2.0 / radius_count))).astype(jnp.bfloat16)
    return synthesis, analysis


def plane_matrices(slots):
    width = 2 * slots * 2
    pair = width // 2
    inner = np.arange(width)
    plane, rest = inner % 2, inner // 2
    gather = np.zeros((width, width), np.float32)
    gather[inner, plane * pair + rest] = 1.0
    eye = np.eye(pair, dtype=np.float32)
    own = np.kron(eye, np.array([[0, 8], [-8, 0]], np.float32))
    low = np.kron(eye, np.array([[1, -8], [0, 1]], np.float32))
    high = np.kron(eye, np.array([[-1, 0], [8, -1]], np.float32))
    rows = np.concatenate([own, low, high], axis=1)
    swap = np.roll(np.eye(width, dtype=np.float32), pair, axis=1)
    both = np.concatenate([gather, gather @ swap], axis=1)
    slope = rows.T @ both
    return (
        rows.astype(jnp.bfloat16),
        both.astype(jnp.bfloat16),
        slope.astype(jnp.bfloat16),
        gather.T.astype(jnp.bfloat16),
    )


def dot(a, b, dims):
    return lax.dot_general(a, b, (dims, ((), ())), preferred_element_type=F32)


def masked_rows(block, lens, weight):
    modes = lax.broadcasted_iota(jnp.int32, block.shape, 1)
    return jnp.where(modes < lens, block.astype(F32) * weight, 0.0)


def field_rows(ref, field):
    block = ref[field]
    return block.reshape(math.prod(block.shape[:-1]), block.shape[-1])


def raw_kernel(x_ref, lens_ref, weight_ref, table_ref, out_ref, held):
    @pl.when(pl.program_id(0) == 0)
    def _():
        for field in range(2):
            rows = masked_rows(field_rows(x_ref, field), lens_ref[...], weight_ref[...])
            held[field * rows.shape[0]:(field + 1) * rows.shape[0], :] = rows.astype(BF16)

    out_ref[...] = dot(table_ref[...], held[...], ((1,), (1,))).astype(BF16)


def slope_kernel(x_ref, low_ref, high_ref, lens_ref, weight_ref, rows_ref, table_ref, out_ref, held):
    @pl.when(pl.program_id(0) == 0)
    def _():
        for field in range(2):
            stacked = jnp.concatenate(
                [field_rows(x_ref, field), field_rows(low_ref, field), field_rows(high_ref, field)],
                axis=0,
            )
            slope = dot(rows_ref[...], stacked, ((1,), (0,)))
            rows = masked_rows(slope, lens_ref[...], weight_ref[...])
            held[field * rows.shape[0]:(field + 1) * rows.shape[0], :] = rows.astype(BF16)

    out_ref[...] = dot(table_ref[...], held[...], ((1,), (1,))).astype(BF16)


def whole(shape):
    return pl.BlockSpec(shape, lambda i: (0,) * len(shape))


def two_fields(shape, first):
    return pl.BlockSpec((2,) + tuple(shape[1:]), lambda i: (first // 2,) + (0,) * (len(shape) - 1))


def radial_raw(x, lens, weight, table, step=256):
    rows, modes = 2 * math.prod(x.shape[1:-1]), x.shape[-1]
    return pl.pallas_call(
        raw_kernel,
        grid=(R // step,),
        out_shape=pltpu.HBM((R, rows), BF16),
        in_specs=[two_fields(x.shape, 2), whole(lens.shape), whole(weight.shape),
                  pl.BlockSpec((step, modes), lambda i: (i, 0))],
        out_specs=pl.BlockSpec((step, rows), lambda i: (i, 0)),
        scratch_shapes=[pltpu.VMEM((rows, modes), BF16)],
        compiler_params=pltpu.CompilerParams(vmem_limit_bytes=16 << 20),
        name="radial_raw",
    )(in_hbm(x), lens, weight, in_hbm(table))


def radial_slope(x, low, high, lens, weight, rows_map, table, step=256):
    rows, modes = 2 * math.prod(x.shape[1:-1]), x.shape[-1]
    return pl.pallas_call(
        slope_kernel,
        grid=(R // step,),
        out_shape=pltpu.HBM((R, rows), BF16),
        in_specs=[two_fields(x.shape, 0), whole(low.shape), whole(high.shape), whole(lens.shape),
                  whole(weight.shape), whole(rows_map.shape),
                  pl.BlockSpec((step, modes), lambda i: (i, 0))],
        out_specs=pl.BlockSpec((step, rows), lambda i: (i, 0)),
        scratch_shapes=[pltpu.VMEM((rows, modes), BF16)],
        compiler_params=pltpu.CompilerParams(vmem_limit_bytes=16 << 20),
        name="radial_slope",
    )(x, low, high, lens, weight, rows_map, table)


def table_kernel(orders_ref, out_ref):
    slots = orders_ref.shape[0]
    points = out_ref.shape[1]
    orders = jnp.broadcast_to(orders_ref[...], (slots, 128))
    lane = lax.broadcasted_iota(jnp.int32, (slots, 128), 1)
    unit = 2.0 * math.pi / points
    fine = ((orders * lane) & (points - 1)).astype(F32) * unit
    turn = ((orders * 128) & (points - 1)).astype(F32) * unit
    cos_now, sin_now = jnp.cos(fine), jnp.sin(fine)
    cos_turn, sin_turn = jnp.cos(turn), jnp.sin(turn)
    for block in range(points // 128):
        part = pl.ds(block * 128, 128)
        out_ref[0:slots, part] = cos_now.astype(BF16)
        out_ref[slots:2 * slots, part] = (-sin_now).astype(BF16)
        cos_now, sin_now = (
            cos_now * cos_turn - sin_now * sin_turn,
            sin_now * cos_turn + cos_now * sin_turn,
        )


def azimuthal_table(orders, groups, slots, points):
    return pl.pallas_call(
        table_kernel,
        grid=(groups,),
        out_shape=pltpu.HBM((groups * 2 * slots, points), BF16),
        in_specs=[pl.BlockSpec((slots, 1), lambda i: (i, 0))],
        out_specs=pl.BlockSpec((2 * slots, points), lambda i: (i, 0)),
        compiler_params=pltpu.CompilerParams(vmem_limit_bytes=8 << 20),
        name="azimuthal_table",
    )(orders)


def place_field(lhs, mapped, row, groups, band):
    width = mapped.shape[1] // 2
    low_lanes = lax.broadcasted_iota(jnp.int32, (band, width), 1) < width // 2
    for pair in range(groups // 2):
        even = mapped[2 * pair * band:(2 * pair + 1) * band]
        odd = mapped[(2 * pair + 1) * band:(2 * pair + 2) * band]
        first = jnp.where(low_lanes, even[:, :width], odd[:, width:])
        second = jnp.where(low_lanes, even[:, width:], odd[:, :width])
        cols = pl.ds(pair * width, width)
        lhs[row:row + band, cols] = first.astype(BF16)
        lhs[row + band:row + 2 * band, cols] = second.astype(BF16)


def axial_kernel(groups, band, raw_ref, low_ref, high_ref, both_ref, dz_ref, table_ref,
                 axial_ref, product_ref, lhs):
    width = both_ref.shape[0]

    @pl.when(pl.program_id(0) == 0)
    def _():
        joined = jnp.concatenate([raw_ref[:, 0:width], low_ref[...], high_ref[...]], axis=1)
        place_field(lhs, dot(joined, dz_ref[...], ((1,), (0,))), 0, groups, band)
        mapped = dot(raw_ref[:, width:2 * width], both_ref[...], ((1,), (0,)))
        place_field(lhs, mapped, 2 * band, groups, band)

    values = dot(lhs[...], table_ref[...], ((1,), (0,)))
    axial = values[2 * band:] * (1.0 / 12.0)
    axial_ref[...] = axial
    product_ref[...] = (values[:2 * band] * axial).astype(BF16)


def axial_stage(raw, low, high, both, dz, table, groups, band, step=512):
    rows, points = table.shape
    columns = pl.BlockSpec((2 * band, step), lambda i: (0, i))
    return pl.pallas_call(
        functools.partial(axial_kernel, groups, band),
        grid=(points // step,),
        out_shape=(jax.ShapeDtypeStruct((2 * band, points), F32),
                   jax.ShapeDtypeStruct((2 * band, points), BF16)),
        in_specs=[whole(raw.shape), whole(low.shape), whole(high.shape),
                  whole(both.shape), whole(dz.shape),
                  pl.BlockSpec((rows, step), lambda i: (0, i))],
        out_specs=(columns, columns),
        scratch_shapes=[pltpu.VMEM((4 * band, rows), BF16)],
        compiler_params=pltpu.CompilerParams(vmem_limit_bytes=20 << 20),
        name="axial_stage",
    )(raw, low, high, both, dz, in_hbm(table))


def physical_kernel(groups, band, scale, slope_ref, axial_ref, product_ref, both_ref,
                    table_ref, out_ref, lhs, acc):
    step = pl.program_id(0)
    width = both_ref.shape[0]
    half = width // 2

    @pl.when(step == 0)
    def _():
        acc[...] = jnp.zeros_like(acc)
        for field in range(2):
            mapped = dot(slope_ref[:, field * width:(field + 1) * width], both_ref[...], ((1,), (0,)))
            place_field(lhs, mapped, 2 * field * band, groups, band)

    values = dot(lhs[...], table_ref[...], ((1,), (0,)))
    axial = axial_ref[...]
    products = jnp.concatenate(
        [(values[:2 * band] * axial).astype(BF16), (values[2 * band:] * axial).astype(BF16),
         product_ref[...]], axis=0
    )
    acc[...] += dot(products, table_ref[...], ((1,), (1,)))

    @pl.when(step == pl.num_programs(0) - 1)
    def _():
        low_lanes = lax.broadcasted_iota(jnp.int32, (band, width), 1) < half
        for g in range(3):
            for pair in range(groups // 2):
                cols = pl.ds(pair * width, width)
                first = acc[(2 * g) * band:(2 * g + 1) * band, cols] * scale
                second = acc[(2 * g + 1) * band:(2 * g + 2) * band, cols] * scale
                even = jnp.where(low_lanes, first, pltpu.roll(second, half, 1))
                odd = jnp.where(low_lanes, pltpu.roll(first, half, 1), second)
                out_cols = pl.ds(g * width, width)
                out_ref[2 * pair * band:(2 * pair + 1) * band, out_cols] = even.astype(BF16)
                out_ref[(2 * pair + 1) * band:(2 * pair + 2) * band, out_cols] = odd.astype(BF16)


def physical_stage(slope, axial, product, both, table, groups, band, step=512):
    rows, points = table.shape
    width = both.shape[0]
    columns = pl.BlockSpec((2 * band, step), lambda i: (0, i))
    return pl.pallas_call(
        functools.partial(physical_kernel, groups, band, math.sqrt(2.0 / points)),
        grid=(points // step,),
        out_shape=jax.ShapeDtypeStruct((groups * band, 3 * width), BF16),
        in_specs=[whole(slope.shape), columns, columns, whole(both.shape),
                  pl.BlockSpec((rows, step), lambda i: (0, i))],
        out_specs=whole((groups * band, 3 * width)),
        scratch_shapes=[pltpu.VMEM((4 * band, rows), BF16), pltpu.VMEM((6 * band, rows), F32)],
        compiler_params=pltpu.CompilerParams(vmem_limit_bytes=24 << 20),
        name="physical_stage",
    )(slope, axial, product, both, in_hbm(table))


def final_kernel(x_ref, lens_ref, back_ref, table_ref, out_ref, held):
    width = back_ref.shape[0]
    step = pl.program_id(0)
    columns = table_ref.shape[1]

    @pl.when(step == 0)
    def _():
        for g in range(3):
            part = slice(g * width, (g + 1) * width)
            held[:, part] = dot(x_ref[:, part], back_ref[...], ((1,), (0,))).astype(BF16)

    result = dot(held[...], table_ref[...], ((0,), (0,)))
    modes = lax.broadcasted_iota(jnp.int32, (width, columns), 1) + step * columns
    keep = modes < lens_ref[...]
    for g in range(3):
        rows = jnp.where(keep, result[g * width:(g + 1) * width], 0.0).astype(BF16)
        out_ref[g] = rows.reshape(out_ref.shape[1:])


def radial_analysis(x, lens, back, table, shape, step=256):
    radii, lanes = x.shape
    modes = table.shape[1]
    return pl.pallas_call(
        final_kernel,
        grid=(modes // step,),
        out_shape=pltpu.HBM(shape, BF16),
        in_specs=[whole(x.shape), whole(lens.shape), whole(back.shape),
                  pl.BlockSpec((radii, step), lambda i: (0, i))],
        out_specs=pl.BlockSpec(tuple(shape[:-1]) + (step,), lambda i: (0, 0, 0, 0, i)),
        scratch_shapes=[pltpu.VMEM((radii, lanes), BF16)],
        compiler_params=pltpu.CompilerParams(vmem_limit_bytes=16 << 20),
        name="radial_analysis",
    )(x, lens, back, table)


def in_hbm(x):
    return pltpu.with_memory_space_constraint(x, pltpu.HBM)


def shift(block, offset):
    count = lax.axis_size("axial")
    return lax.ppermute(block, "axial", [(i, (i + offset) % count) for i in range(count)])


def exchange(block):
    return lax.all_to_all(block, "order", split_axis=0, concat_axis=0, tiled=True)


def shards(coefficients, order_lists, lengths):
    field_count, part_count, slots, planes, modes = coefficients.shape
    order_count = order_lists.shape[0]
    points = 2 * order_count
    groups = lax.axis_size("order")
    band = R // groups
    width = part_count * slots * planes
    synthesis, analysis = radial_constants(R, modes)
    rows_map, both, dz, back = plane_matrices(slots)

    sloped = coefficients[:2]
    low, high = shift(sloped, 1), shift(sloped, -1)

    owned = lax.dynamic_slice_in_dim(order_lists, lax.axis_index("order") * slots, slots)
    catalog = jnp.arange(order_count, dtype=jnp.int32)
    own_lengths = jnp.sum(
        jnp.where(owned[:, None] == catalog[None, :], lengths[None, :], 0), axis=1
    )
    spread = (part_count, slots, planes)
    lens = jnp.broadcast_to(own_lengths[None, :, None], spread).reshape(width, 1)
    weight = jnp.where(owned == 0, 1.0, 2.0).astype(F32)
    weight = jnp.broadcast_to(weight[None, :, None], spread).reshape(width, 1)

    raw_bands = exchange(radial_raw(coefficients, lens, weight, synthesis))
    table = azimuthal_table(order_lists.reshape(order_count, 1), groups, slots, points)
    own_band = raw_bands[:, :width]
    low_band, high_band = shift(own_band, 1), shift(own_band, -1)
    later_lens, table = lax.optimization_barrier((lens, table))
    slope_bands = exchange(
        radial_slope(coefficients, low, high, later_lens, weight, rows_map, synthesis)
    )
    axial, product = axial_stage(raw_bands, low_band, high_band, both, dz, table, groups, band)
    spectral = physical_stage(slope_bands, axial, product, both, table, groups, band)
    shape = (3, part_count, slots, planes, modes)
    return radial_analysis(exchange(spectral), lens, back, analysis, shape)


def solution(mesh):
    placed = (P(None, None, "order", "axial", None), P(), P())
    return jax.shard_map(
        shards,
        mesh=mesh,
        in_specs=placed,
        out_specs=P(None, None, "order", "axial", None),
        check_vma=False,
    )
```

```python
import functools
import math

import jax
import jax.numpy as jnp
import numpy as np
from jax import lax
from jax.experimental import pallas as pl
from jax.experimental.pallas import tpu as pltpu
from jax.sharding import PartitionSpec as P

R = 1024
F32 = jnp.float32
BF16 = jnp.bfloat16


def radial_constants(radius_count, mode_count):
    radius_ids = np.arange(radius_count)
    mode_ids = np.arange(mode_count)
    phases = mode_ids[None, :] * (2 * radius_ids[:, None] + 1) % (4 * radius_count)
    cosines = np.cos(phases * (math.pi / (2 * radius_count))).astype(np.float32)
    synthesis = cosines.astype(jnp.bfloat16)
    analysis = (cosines * np.float32(math.sqrt(2.0 / radius_count))).astype(jnp.bfloat16)
    return synthesis, analysis


def plane_matrices(slots):
    width = 2 * slots * 2
    pair = width // 2
    inner = np.arange(width)
    plane, rest = inner % 2, inner // 2
    gather = np.zeros((width, width), np.float32)
    gather[inner, plane * pair + rest] = 1.0
    eye = np.eye(pair, dtype=np.float32)
    own = np.kron(eye, np.array([[0, 8], [-8, 0]], np.float32))
    low = np.kron(eye, np.array([[1, -8], [0, 1]], np.float32))
    high = np.kron(eye, np.array([[-1, 0], [8, -1]], np.float32))
    rows = np.concatenate([own, low, high], axis=1)
    swap = np.roll(np.eye(width, dtype=np.float32), pair, axis=1)
    both = np.concatenate([gather, gather @ swap], axis=1)
    slope = rows.T @ both
    return (
        rows.astype(jnp.bfloat16),
        both.astype(jnp.bfloat16),
        slope.astype(jnp.bfloat16),
        gather.T.astype(jnp.bfloat16),
    )


def dot(a, b, dims):
    return lax.dot_general(a, b, (dims, ((), ())), preferred_element_type=F32)


HERE = pl.BlockSpec(memory_space=pltpu.VMEM)
FAR = pl.BlockSpec(memory_space=pltpu.HBM)
SCALARS = pl.BlockSpec(memory_space=pltpu.SMEM)


def in_hbm(x):
    return pltpu.with_memory_space_constraint(x, pltpu.HBM)


def call(kernel, name, out_shape, in_specs, out_specs, scratch=(), limit=16):
    return pl.pallas_call(
        kernel,
        out_shape=out_shape,
        in_specs=in_specs,
        out_specs=out_specs,
        scratch_shapes=list(scratch),
        compiler_params=pltpu.CompilerParams(vmem_limit_bytes=limit << 20),
        name=name,
    )


def stage_kernel(x_ref, slope_ref, raw_ref, sem):
    copies = []
    for field in range(4):
        target = slope_ref if field < 2 else raw_ref
        for part in range(2):
            copies.append(pltpu.make_async_copy(
                x_ref.at[field, part], target.at[field % 2, part], sem.at[2 * field + part]))
    for copy in copies:
        copy.start()
    for copy in copies:
        copy.wait()


def stage(x):
    half = (2,) + x.shape[1:]
    return call(
        stage_kernel, "stage",
        (pltpu.VMEM(half, BF16), pltpu.VMEM(half, BF16)),
        [FAR], (HERE, HERE), [pltpu.SemaphoreType.DMA((8,))],
    )(in_hbm(x))


def field_rows(ref, field):
    block = ref[field]
    return block.reshape(math.prod(block.shape[:-1]), block.shape[-1])


def masked_rows(block, lens, weight):
    modes = lax.broadcasted_iota(jnp.int32, block.shape, 1)
    return jnp.where(modes < lens[:, :1], block.astype(F32) * weight[:, :1], 0.0).astype(BF16)


def send_bands(table_ref, rows, out_ref, buffer, sem, loads=None, count=4):
    size = table_ref.shape[0] // count
    copies = []
    for i in range(count):
        part = pl.ds(i * size, size)
        if loads is not None:
            loads[i].wait()
        buffer[part, :] = dot(table_ref[part, :], rows, ((1,), (1,))).astype(BF16)
        copies.append(pltpu.make_async_copy(buffer.at[part], out_ref.at[part], sem.at[i]))
        copies[-1].start()
    for copy in copies:
        copy.wait()


def raw_kernel(slots, orders_ref, lengths_ref, x_ref, table_ref, out_ref, lens_ref, weight_ref,
               buffer, sem, held_table, load_sem):
    size = held_table.shape[0] // 4
    loads = [
        pltpu.make_async_copy(table_ref.at[pl.ds(i * size, size)],
                              held_table.at[pl.ds(i * size, size)], load_sem.at[i])
        for i in range(4)
    ]
    for load in loads:
        load.start()
    base = lax.axis_index("order") * slots
    rows = 2 * slots
    slot_of = lax.broadcasted_iota(jnp.int32, (rows, 128), 0) // 2
    lens = jnp.zeros((rows, 128), jnp.int32)
    order = jnp.zeros((rows, 128), jnp.int32)
    for slot in range(slots):
        here = orders_ref[base + slot]
        lens = jnp.where(slot_of == slot, lengths_ref[here], lens)
        order = jnp.where(slot_of == slot, here, order)
    lens = jnp.concatenate([lens, lens], axis=0)
    weight = jnp.where(order == 0, 1.0, 2.0).astype(F32)
    weight = jnp.concatenate([weight, weight], axis=0)
    lens_ref[...] = lens
    weight_ref[...] = weight
    held = [masked_rows(field_rows(x_ref, field), lens, weight) for field in range(2)]
    send_bands(held_table, jnp.concatenate(held, axis=0), out_ref, buffer, sem, loads)


def radial_raw(orders, lengths, x, table):
    rows = 2 * math.prod(x.shape[1:-1])
    return call(
        functools.partial(raw_kernel, x.shape[2]), "radial_raw",
        (pltpu.HBM((R, rows), BF16),
         jax.ShapeDtypeStruct((rows // 2, 128), jnp.int32),
         jax.ShapeDtypeStruct((rows // 2, 128), F32)),
        [SCALARS, SCALARS, HERE, FAR], (FAR, HERE, HERE),
        [pltpu.VMEM((R, rows), BF16), pltpu.SemaphoreType.DMA((4,)),
         pltpu.VMEM(table.shape, BF16), pltpu.SemaphoreType.DMA((4,))],
    )(orders, lengths, x, in_hbm(table))


def slope_kernel(x_ref, low_ref, high_ref, lens_ref, weight_ref, rows_ref, table_ref, out_ref,
                 buffer, sem):
    held = []
    for field in range(2):
        stacked = jnp.concatenate(
            [field_rows(x_ref, field), field_rows(low_ref, field), field_rows(high_ref, field)],
            axis=0,
        )
        slope = dot(rows_ref[...], stacked, ((1,), (0,)))
        held.append(masked_rows(slope, lens_ref[...], weight_ref[...]))
    send_bands(table_ref, jnp.concatenate(held, axis=0), out_ref, buffer, sem)


def radial_slope(x, low, high, lens, weight, rows_map, table):
    rows = 2 * math.prod(x.shape[1:-1])
    return call(
        slope_kernel, "radial_slope", pltpu.HBM((R, rows), BF16), [HERE] * 7, FAR,
        [pltpu.VMEM((R, rows), BF16), pltpu.SemaphoreType.DMA((4,))],
    )(x, low, high, lens, weight, rows_map, table)


def sine_cosine(phase, points):
    centred = ((phase + points // 2) & (points - 1)) - points // 2
    y = centred.astype(F32) * (math.pi / points)
    square = y * y
    sine = jnp.float32(0.0)
    for n in (11, 9, 7, 5, 3, 1):
        sine = sine * square + (-1.0) ** (n // 2) / math.factorial(n)
    sine = sine * y
    cosine = jnp.float32(0.0)
    for n in (12, 10, 8, 6, 4, 2, 0):
        cosine = cosine * square + (-1.0) ** (n // 2) / math.factorial(n)
    return 1.0 - 2.0 * sine * sine, 2.0 * sine * cosine


def table_kernel(slots, orders_ref, out_ref):
    points = out_ref.shape[1]
    lane = lax.broadcasted_iota(jnp.int32, (slots, 128), 1)
    per_row = 128 // slots
    for row in range(orders_ref.shape[0]):
        column = jnp.broadcast_to(orders_ref[row:row + 1, :], (128, 128)).T
        for piece in range(per_row):
            orders = column[piece * slots:(piece + 1) * slots]
            start = (row * per_row + piece) * 2 * slots
            cos_now, sin_now = sine_cosine((orders * lane) & (points - 1), points)
            cos_turn, sin_turn = sine_cosine((orders * 128) & (points - 1), points)
            for block in range(points // 128):
                part = pl.ds(block * 128, 128)
                out_ref[start:start + slots, part] = cos_now.astype(BF16)
                out_ref[start + slots:start + 2 * slots, part] = (-sin_now).astype(BF16)
                cos_now, sin_now = (
                    cos_now * cos_turn - sin_now * sin_turn,
                    sin_now * cos_turn + cos_now * sin_turn,
                )


def azimuthal_table(orders, slots, points):
    return call(
        functools.partial(table_kernel, slots), "azimuthal_table",
        pltpu.VMEM((2 * orders.size, points), BF16), [HERE], HERE,
    )(orders)


def place_field(lhs, mapped, row, groups, band):
    width = mapped.shape[1] // 2
    low_lanes = lax.broadcasted_iota(jnp.int32, (band, width), 1) < width // 2
    for pair in range(groups // 2):
        even = mapped[2 * pair * band:(2 * pair + 1) * band]
        odd = mapped[(2 * pair + 1) * band:(2 * pair + 2) * band]
        first = jnp.where(low_lanes, even[:, :width], odd[:, width:])
        second = jnp.where(low_lanes, even[:, width:], odd[:, :width])
        cols = pl.ds(pair * width, width)
        lhs[row:row + band, cols] = first.astype(BF16)
        lhs[row + band:row + 2 * band, cols] = second.astype(BF16)


def axial_kernel(groups, band, step, raw_ref, low_ref, high_ref, both_ref, dz_ref, table_ref,
                 axial_ref, product_ref, lhs):
    width = both_ref.shape[0]
    joined = jnp.concatenate([raw_ref[:, 0:width], low_ref[...], high_ref[...]], axis=1)
    place_field(lhs, dot(joined, dz_ref[...], ((1,), (0,))), 0, groups, band)
    mapped = dot(raw_ref[:, width:2 * width], both_ref[...], ((1,), (0,)))
    place_field(lhs, mapped, 2 * band, groups, band)
    for start in range(0, table_ref.shape[1], step):
        part = pl.ds(start, step)
        values = dot(lhs[...], table_ref[:, part], ((1,), (0,)))
        axial = values[2 * band:] * (1.0 / 12.0)
        axial_ref[:, part] = axial
        product_ref[:, part] = (values[:2 * band] * axial).astype(BF16)


def axial_stage(raw, low, high, both, dz, table, groups, band, step=512):
    rows, points = table.shape
    return call(
        functools.partial(axial_kernel, groups, band, step), "axial_stage",
        (jax.ShapeDtypeStruct((2 * band, points), F32),
         jax.ShapeDtypeStruct((2 * band, points), BF16)),
        [HERE] * 6, (HERE, HERE), [pltpu.VMEM((4 * band, rows), BF16)],
    )(raw, low, high, both, dz, table)


def physical_kernel(groups, band, step, scale, slope_ref, axial_ref, product_ref, both_ref,
                    far_ref, out_ref, lhs, products, table_ref, sem):
    width = both_ref.shape[0]
    half = width // 2
    rows, points = table_ref.shape
    loads = []
    for block in range(points // step):
        for piece in range(4):
            area = (pl.ds(piece * (rows // 4), rows // 4), pl.ds(block * step, step))
            loads.append(pltpu.make_async_copy(
                far_ref.at[area], table_ref.at[area], sem.at[4 * block + piece]))
            loads[-1].start()
    for field in range(2):
        mapped = dot(slope_ref[:, field * width:(field + 1) * width], both_ref[...], ((1,), (0,)))
        place_field(lhs, mapped, 2 * field * band, groups, band)
    products[4 * band:6 * band, :] = product_ref[...]
    for start in range(0, points, step):
        part = pl.ds(start, step)
        for piece in range(4):
            loads[4 * (start // step) + piece].wait()
        values = dot(lhs[...], table_ref[:, part], ((1,), (0,)))
        axial = axial_ref[:, part]
        products[0:2 * band, part] = (values[:2 * band] * axial).astype(BF16)
        products[2 * band:4 * band, part] = (values[2 * band:] * axial).astype(BF16)

    low_lanes = lax.broadcasted_iota(jnp.int32, (band, width), 1) < half
    for start in range(0, rows, step):
        part = pl.ds(start, step)
        spectral = dot(products[...], table_ref[part, :], ((1,), (1,))) * scale
        for g in range(3):
            out_cols = pl.ds(g * width, width)
            for tile in range(step // width):
                cols = slice(tile * width, (tile + 1) * width)
                first = spectral[(2 * g) * band:(2 * g + 1) * band, cols]
                second = spectral[(2 * g + 1) * band:(2 * g + 2) * band, cols]
                even = jnp.where(low_lanes, first, pltpu.roll(second, half, 1))
                odd = jnp.where(low_lanes, pltpu.roll(first, half, 1), second)
                row = (start // width + tile) * 2 * band
                out_ref[row:row + band, out_cols] = even.astype(BF16)
                out_ref[row + band:row + 2 * band, out_cols] = odd.astype(BF16)


def physical_stage(slope, axial, product, both, table, groups, band, step=512):
    rows, points = table.shape
    width = both.shape[0]
    return call(
        functools.partial(physical_kernel, groups, band, step, math.sqrt(2.0 / points)),
        "physical_stage",
        jax.ShapeDtypeStruct((groups * band, 3 * width), BF16), [HERE] * 4 + [FAR], HERE,
        [pltpu.VMEM((4 * band, rows), BF16), pltpu.VMEM((6 * band, points), BF16),
         pltpu.VMEM(table.shape, BF16), pltpu.SemaphoreType.DMA((4 * (points // step),))],
        limit=28,
    )(slope, axial, product, both, in_hbm(table))


def final_kernel(x_ref, lens_ref, back_ref, table_ref, out_ref, buffer, sem):
    width = back_ref.shape[0]
    modes = lax.broadcasted_iota(jnp.int32, (width, table_ref.shape[1]), 1)
    keep = modes < lens_ref[:, :1]
    copies = []
    for g in range(3):
        mapped = dot(x_ref[:, g * width:(g + 1) * width], back_ref[...], ((1,), (0,)))
        result = dot(mapped.astype(BF16), table_ref[...], ((0,), (0,)))
        rows = jnp.where(keep, result, 0.0).astype(BF16)
        buffer[g] = rows.reshape(buffer.shape[1:])
        copies.append(pltpu.make_async_copy(buffer.at[g], out_ref.at[g], sem.at[g]))
        copies[-1].start()
    for copy in copies:
        copy.wait()


def radial_analysis(x, lens, back, table, shape):
    return call(
        final_kernel, "radial_analysis", pltpu.HBM(shape, BF16), [HERE] * 4, FAR,
        [pltpu.VMEM(shape, BF16), pltpu.SemaphoreType.DMA((3,))],
    )(x, lens, back, table)


def shift(block, offset):
    count = lax.axis_size("axial")
    return lax.ppermute(block, "axial", [(i, (i + offset) % count) for i in range(count)])


def exchange(block):
    return lax.all_to_all(block, "order", split_axis=0, concat_axis=0, tiled=True)


def shards(coefficients, order_lists, lengths):
    field_count, part_count, slots, planes, modes = coefficients.shape
    order_count = order_lists.shape[0]
    points = 2 * order_count
    groups = lax.axis_size("order")
    band = R // groups
    width = part_count * slots * planes
    synthesis, analysis = radial_constants(R, modes)
    rows_map, both, dz, back = plane_matrices(slots)

    sloped, raw = stage(coefficients)
    low, high = shift(sloped, 1), shift(sloped, -1)
    bands, lens, weight = radial_raw(order_lists, lengths, raw, synthesis)
    raw_bands = exchange(bands)
    table = azimuthal_table(order_lists.reshape(order_count // 128, 128), slots, points)
    own_band = raw_bands[:, :width]
    low_band, high_band = shift(own_band, 1), shift(own_band, -1)
    later_lens, table = lax.optimization_barrier((lens, table))
    slope_bands = exchange(
        radial_slope(sloped, low, high, later_lens, weight, rows_map, synthesis)
    )
    axial, product = axial_stage(raw_bands, low_band, high_band, both, dz, table, groups, band)
    spectral = physical_stage(slope_bands, axial, product, both, table, groups, band)
    shape = (3, part_count, slots, planes, modes)
    return radial_analysis(exchange(spectral), lens, back, analysis, shape)


def solution(mesh):
    placed = (P(None, None, "order", "axial", None), P(), P())
    return jax.shard_map(
        shards,
        mesh=mesh,
        in_specs=placed,
        out_specs=P(None, None, "order", "axial", None),
        check_vma=False,
    )
```

```python
import functools
import math

import jax
import jax.numpy as jnp
import numpy as np
from jax import lax
from jax.experimental import pallas as pl
from jax.experimental.pallas import tpu as pltpu
from jax.sharding import PartitionSpec as P

R = 1024
F32 = jnp.float32
BF16 = jnp.bfloat16


def radial_constants(radius_count, mode_count):
    radius_ids = np.arange(radius_count)
    mode_ids = np.arange(mode_count)
    phases = mode_ids[None, :] * (2 * radius_ids[:, None] + 1) % (4 * radius_count)
    cosines = np.cos(phases * (math.pi / (2 * radius_count))).astype(np.float32)
    synthesis = cosines.astype(jnp.bfloat16)
    analysis = (cosines * np.float32(math.sqrt(2.0 / radius_count))).astype(jnp.bfloat16)
    return synthesis, analysis


def plane_matrices(slots):
    width = 2 * slots * 2
    pair = width // 2
    inner = np.arange(width)
    plane, rest = inner % 2, inner // 2
    gather = np.zeros((width, width), np.float32)
    gather[inner, plane * pair + rest] = 1.0
    eye = np.eye(pair, dtype=np.float32)
    own = np.kron(eye, np.array([[0, 8], [-8, 0]], np.float32))
    low = np.kron(eye, np.array([[1, -8], [0, 1]], np.float32))
    high = np.kron(eye, np.array([[-1, 0], [8, -1]], np.float32))
    rows = np.concatenate([own, low, high], axis=1)
    swap = np.roll(np.eye(width, dtype=np.float32), pair, axis=1)
    both = np.concatenate([gather, gather @ swap], axis=1)
    return (
        rows.astype(jnp.bfloat16),
        both.astype(jnp.bfloat16),
        gather.T.astype(jnp.bfloat16),
    )


def dot(a, b, dims):
    return lax.dot_general(a, b, (dims, ((), ())), preferred_element_type=F32)


HERE = pl.BlockSpec(memory_space=pltpu.VMEM)
FAR = pl.BlockSpec(memory_space=pltpu.HBM)
SCALARS = pl.BlockSpec(memory_space=pltpu.SMEM)


def in_hbm(x):
    return pltpu.with_memory_space_constraint(x, pltpu.HBM)


def call(kernel, name, out_shape, in_specs, out_specs, scratch=(), limit=16):
    return pl.pallas_call(
        kernel,
        out_shape=out_shape,
        in_specs=in_specs,
        out_specs=out_specs,
        scratch_shapes=list(scratch),
        compiler_params=pltpu.CompilerParams(vmem_limit_bytes=limit << 20),
        name=name,
    )


def stage_kernel(x_ref, out_ref, sem):
    fields, parts, slots = out_ref.shape[:3]
    copies = []
    for field in range(fields):
        for part in range(parts):
            for half in range(2):
                area = (field, part, pl.ds(half * (slots // 2), slots // 2))
                copies.append(pltpu.make_async_copy(
                    x_ref.at[area], out_ref.at[area], sem.at[len(copies)]))
                copies[-1].start()
    for copy in copies:
        copy.wait()


def stage(x):
    return call(
        stage_kernel, "stage", pltpu.VMEM((3,) + x.shape[1:], BF16),
        [FAR], HERE, [pltpu.SemaphoreType.DMA((12,))],
    )(in_hbm(x))


def field_rows(ref, field):
    block = ref[field]
    return block.reshape(math.prod(block.shape[:-1]), block.shape[-1])


def masked_rows(block, lens, weight):
    modes = lax.broadcasted_iota(jnp.int32, block.shape, 1)
    return jnp.where(modes < lens[:, :1], block.astype(F32) * weight[:, :1], 0.0).astype(BF16)


def send_bands(table_ref, rows, out_ref, buffer, sem, loads=None, count=4):
    size = table_ref.shape[0] // count
    copies = []
    for i in range(count):
        part = pl.ds(i * size, size)
        if loads is not None:
            loads[i].wait()
        buffer[part, :] = dot(table_ref[part, :], rows, ((1,), (1,))).astype(BF16)
        copies.append(pltpu.make_async_copy(buffer.at[part], out_ref.at[part], sem.at[i]))
        copies[-1].start()
    for copy in copies:
        copy.wait()


def slot_rows(orders, lengths, slots):
    index = lax.axis_index("order")
    per_row = 128 // slots
    lane = lax.broadcasted_iota(jnp.int32, (128, 128), 1)
    held = jnp.broadcast_to(orders[pl.ds(index // per_row, 1), :], (128, 128)).T
    total = jnp.zeros((128, 128), F32)
    for row in range(lengths.shape[0]):
        wide = jnp.broadcast_to(lengths[row:row + 1, :], (128, 128)).astype(F32)
        total += jnp.where(held == lane + row * 128, wide, 0.0)
    found = jnp.sum(total, axis=1, keepdims=True).astype(jnp.int32)
    found = jnp.broadcast_to(found, (128, 128))
    zero = jnp.where(held == 0, 1, 0)
    columns = jnp.where(lane == 0, found >> 3, jnp.where(lane == 1, found & 7, zero))
    rows = lax.broadcasted_iota(jnp.int32, (2 * slots, 128), 0) // 2
    picked = lax.broadcasted_iota(jnp.int32, (2 * slots, 128), 1)
    pick = jnp.where(picked == rows + (index % per_row) * slots, 1.0, 0.0).astype(BF16)
    result = dot(pick, columns.astype(F32).astype(BF16), ((1,), (0,)))
    lens = (result[:, 0:1] * 8.0 + result[:, 1:2]).astype(jnp.int32)
    weight = 2.0 - result[:, 2:3]
    return jnp.concatenate([lens, lens], axis=0), jnp.concatenate([weight, weight], axis=0)


def raw_kernel(orders_far, lengths_far, x_far, table_far, out_ref, lens_ref, weight_ref,
               buffer, sem, orders, lengths, x_ref, small_sem, table, load_sem):
    size = table.shape[0] // 4
    small = [
        pltpu.make_async_copy(orders_far, orders, small_sem.at[0]),
        pltpu.make_async_copy(lengths_far, lengths, small_sem.at[1]),
        pltpu.make_async_copy(x_far.at[3, 0], x_ref.at[0], small_sem.at[2]),
        pltpu.make_async_copy(x_far.at[3, 1], x_ref.at[1], small_sem.at[3]),
    ]
    loads = [
        pltpu.make_async_copy(table_far.at[pl.ds(i * size, size)],
                              table.at[pl.ds(i * size, size)], load_sem.at[i])
        for i in range(4)
    ]
    for copy in small + loads:
        copy.start()
    small[0].wait()
    small[1].wait()
    lens, weight = slot_rows(orders, lengths, x_ref.shape[1])
    lens_ref[...] = jnp.broadcast_to(lens, lens_ref.shape)
    weight_ref[...] = jnp.broadcast_to(weight, weight_ref.shape)
    small[2].wait()
    small[3].wait()
    block = x_ref[...]
    block = block.reshape(math.prod(block.shape[:-1]), block.shape[-1])
    send_bands(table, masked_rows(block, lens, weight), out_ref, buffer, sem, loads)


def radial_raw(orders, lengths, x, table):
    rows = math.prod(x.shape[1:-1])
    return call(
        raw_kernel, "radial_raw",
        (pltpu.HBM((R, rows), BF16),
         jax.ShapeDtypeStruct((rows, 128), jnp.int32),
         jax.ShapeDtypeStruct((rows, 128), F32)),
        [FAR] * 4, (FAR, HERE, HERE),
        [pltpu.VMEM((R, rows), BF16), pltpu.SemaphoreType.DMA((4,)),
         pltpu.VMEM(orders.shape, jnp.int32), pltpu.VMEM(lengths.shape, jnp.int32),
         pltpu.VMEM(x.shape[1:], BF16), pltpu.SemaphoreType.DMA((4,)),
         pltpu.VMEM(table.shape, BF16), pltpu.SemaphoreType.DMA((4,))],
    )(in_hbm(orders), in_hbm(lengths), in_hbm(x), in_hbm(table))


def slope_kernel(x_ref, low_ref, high_ref, lens_ref, weight_ref, rows_ref, table_ref, out_ref,
                 buffer, sem):
    held = []
    for field in range(3):
        stacked = jnp.concatenate(
            [field_rows(x_ref, field), field_rows(low_ref, field), field_rows(high_ref, field)],
            axis=0,
        )
        slope = dot(rows_ref[...], stacked, ((1,), (0,)))
        held.append(masked_rows(slope, lens_ref[...], weight_ref[...]))
    send_bands(table_ref, jnp.concatenate(held, axis=0), out_ref, buffer, sem)


def radial_slope(x, low, high, lens, weight, rows_map, table):
    rows = math.prod(x.shape[:-1])
    return call(
        slope_kernel, "radial_slope", pltpu.HBM((R, rows), BF16), [HERE] * 7, FAR,
        [pltpu.VMEM((R, rows), BF16), pltpu.SemaphoreType.DMA((4,))],
    )(x, low, high, lens, weight, rows_map, table)


def sine_cosine(phase, points):
    centred = ((phase + points // 2) & (points - 1)) - points // 2
    y = centred.astype(F32) * (math.pi / points)
    square = y * y
    sine = jnp.float32(0.0)
    for n in (11, 9, 7, 5, 3, 1):
        sine = sine * square + (-1.0) ** (n // 2) / math.factorial(n)
    sine = sine * y
    cosine = jnp.float32(0.0)
    for n in (12, 10, 8, 6, 4, 2, 0):
        cosine = cosine * square + (-1.0) ** (n // 2) / math.factorial(n)
    return 1.0 - 2.0 * sine * sine, 2.0 * sine * cosine


def table_kernel(slots, orders_ref, far_ref, out_ref, sem):
    points = out_ref.shape[1]
    copies = []
    lane = lax.broadcasted_iota(jnp.int32, (slots, 128), 1)
    per_row = 128 // slots
    for row in range(orders_ref.shape[0]):
        column = jnp.broadcast_to(orders_ref[row:row + 1, :], (128, 128)).T
        for piece in range(per_row):
            orders = column[piece * slots:(piece + 1) * slots]
            start = (row * per_row + piece) * 2 * slots
            cos_now, sin_now = sine_cosine((orders * lane) & (points - 1), points)
            cos_turn, sin_turn = sine_cosine((orders * 128) & (points - 1), points)
            for block in range(points // 128):
                part = pl.ds(block * 128, 128)
                out_ref[start:start + slots, part] = cos_now.astype(BF16)
                out_ref[start + slots:start + 2 * slots, part] = (-sin_now).astype(BF16)
                cos_now, sin_now = (
                    cos_now * cos_turn - sin_now * sin_turn,
                    sin_now * cos_turn + cos_now * sin_turn,
                )
        part = pl.ds(row * 256, 256)
        copies.append(pltpu.make_async_copy(out_ref.at[part], far_ref.at[part], sem.at[row]))
        copies[-1].start()
    for copy in copies:
        copy.wait()


def azimuthal_table(orders, slots, points):
    return call(
        functools.partial(table_kernel, slots), "azimuthal_table",
        pltpu.HBM((2 * orders.size, points), BF16), [HERE], FAR,
        [pltpu.VMEM((2 * orders.size, points), BF16),
         pltpu.SemaphoreType.DMA((orders.shape[0],))],
    )(orders)


def place_field(lhs, mapped, row, groups, band):
    width = mapped.shape[1] // 2
    low_lanes = lax.broadcasted_iota(jnp.int32, (band, width), 1) < width // 2
    for pair in range(groups // 2):
        even = mapped[2 * pair * band:(2 * pair + 1) * band]
        odd = mapped[(2 * pair + 1) * band:(2 * pair + 2) * band]
        first = jnp.where(low_lanes, even[:, :width], odd[:, width:])
        second = jnp.where(low_lanes, even[:, width:], odd[:, :width])
        cols = pl.ds(pair * width, width)
        lhs[row:row + band, cols] = first.astype(BF16)
        lhs[row + band:row + 2 * band, cols] = second.astype(BF16)


def table_loads(far_ref, table_ref, sem, step):
    rows, points = table_ref.shape
    loads = []
    for block in range(points // step):
        loads.append([])
        for piece in range(4):
            area = (pl.ds(piece * (rows // 4), rows // 4), pl.ds(block * step, step))
            loads[-1].append(pltpu.make_async_copy(
                far_ref.at[area], table_ref.at[area], sem.at[4 * block + piece]))
            loads[-1][-1].start()
    return loads


def axial_kernel(groups, band, step, raw_ref, both_ref, far_ref, axial_ref, lhs, table_ref, sem):
    loads = table_loads(far_ref, table_ref, sem, step)
    place_field(lhs, dot(raw_ref[...], both_ref[...], ((1,), (0,))), 0, groups, band)
    for block in range(table_ref.shape[1] // step):
        part = pl.ds(block * step, step)
        for load in loads[block]:
            load.wait()
        axial_ref[:, part] = dot(lhs[...], table_ref[:, part], ((1,), (0,))) * (1.0 / 12.0)


def axial_stage(raw, both, table, groups, band, step=512):
    rows, points = table.shape
    return call(
        functools.partial(axial_kernel, groups, band, step), "axial_stage",
        jax.ShapeDtypeStruct((2 * band, points), F32),
        [HERE, HERE, FAR], HERE,
        [pltpu.VMEM((2 * band, rows), BF16), pltpu.VMEM(table.shape, BF16),
         pltpu.SemaphoreType.DMA((4 * (points // step),))],
        limit=20,
    )(raw, both, in_hbm(table))


def physical_kernel(groups, band, step, scale, slope_ref, axial_ref, both_ref, far_ref, out_ref,
                    lhs, products, table_ref, sem):
    width = both_ref.shape[0]
    half = width // 2
    rows, points = table_ref.shape
    loads = table_loads(far_ref, table_ref, sem, step)
    for field in range(3):
        mapped = dot(slope_ref[:, field * width:(field + 1) * width], both_ref[...], ((1,), (0,)))
        place_field(lhs, mapped, 2 * field * band, groups, band)
    for block in range(points // step):
        part = pl.ds(block * step, step)
        for load in loads[block]:
            load.wait()
        values = dot(lhs[...], table_ref[:, part], ((1,), (0,)))
        axial = axial_ref[:, part]
        for g in range(3):
            area = slice(2 * g * band, (2 * g + 2) * band)
            products[area, part] = (values[area] * axial).astype(BF16)

    low_lanes = lax.broadcasted_iota(jnp.int32, (band, width), 1) < half
    for start in range(0, rows, step):
        part = pl.ds(start, step)
        spectral = dot(products[...], table_ref[part, :], ((1,), (1,))) * scale
        for g in range(3):
            out_cols = pl.ds(g * width, width)
            for tile in range(step // width):
                cols = slice(tile * width, (tile + 1) * width)
                first = spectral[(2 * g) * band:(2 * g + 1) * band, cols]
                second = spectral[(2 * g + 1) * band:(2 * g + 2) * band, cols]
                even = jnp.where(low_lanes, first, pltpu.roll(second, half, 1))
                odd = jnp.where(low_lanes, pltpu.roll(first, half, 1), second)
                row = (start // width + tile) * 2 * band
                out_ref[row:row + band, out_cols] = even.astype(BF16)
                out_ref[row + band:row + 2 * band, out_cols] = odd.astype(BF16)


def physical_stage(slope, axial, both, table, groups, band, step=512):
    rows, points = table.shape
    width = both.shape[0]
    return call(
        functools.partial(physical_kernel, groups, band, step, math.sqrt(2.0 / points)),
        "physical_stage",
        jax.ShapeDtypeStruct((groups * band, 3 * width), BF16), [HERE] * 3 + [FAR], HERE,
        [pltpu.VMEM((6 * band, rows), BF16), pltpu.VMEM((6 * band, points), BF16),
         pltpu.VMEM(table.shape, BF16), pltpu.SemaphoreType.DMA((4 * (points // step),))],
        limit=28,
    )(slope, axial, both, in_hbm(table))


def final_kernel(x_ref, lens_ref, back_ref, table_ref, out_ref, buffer, sem):
    width = back_ref.shape[0]
    modes = lax.broadcasted_iota(jnp.int32, (width, table_ref.shape[1]), 1)
    keep = modes < lens_ref[:, :1]
    copies = []
    for g in range(3):
        mapped = dot(x_ref[:, g * width:(g + 1) * width], back_ref[...], ((1,), (0,)))
        result = dot(mapped.astype(BF16), table_ref[...], ((0,), (0,)))
        rows = jnp.where(keep, result, 0.0).astype(BF16)
        buffer[g] = rows.reshape(buffer.shape[1:])
        copies.append(pltpu.make_async_copy(buffer.at[g], out_ref.at[g], sem.at[g]))
        copies[-1].start()
    for copy in copies:
        copy.wait()


def radial_analysis(x, lens, back, table, shape):
    return call(
        final_kernel, "radial_analysis", pltpu.HBM(shape, BF16), [HERE] * 4, FAR,
        [pltpu.VMEM(shape, BF16), pltpu.SemaphoreType.DMA((3,))],
    )(x, lens, back, table)


def shift(block, offset):
    count = lax.axis_size("axial")
    return lax.ppermute(block, "axial", [(i, (i + offset) % count) for i in range(count)])


def exchange(block):
    return lax.all_to_all(block, "order", split_axis=0, concat_axis=0, tiled=True)


def shards(coefficients, order_lists, lengths):
    field_count, part_count, slots, planes, modes = coefficients.shape
    order_count = order_lists.shape[0]
    points = 2 * order_count
    groups = lax.axis_size("order")
    band = R // groups
    width = part_count * slots * planes
    synthesis, analysis = radial_constants(R, modes)
    rows_map, both, back = plane_matrices(slots)

    sloped = stage(coefficients)
    low, high = shift(sloped, 1), shift(sloped, -1)
    orders = order_lists.reshape(order_count // 128, 128)
    bands, lens, weight = radial_raw(
        orders, lengths.reshape(order_count // 128, 128), coefficients, synthesis
    )
    raw_bands = exchange(bands)
    table = azimuthal_table(orders, slots, points)
    later_lens, table = lax.optimization_barrier((lens, table))
    slope_bands = exchange(
        radial_slope(sloped, low, high, later_lens, weight, rows_map, synthesis)
    )
    axial = axial_stage(raw_bands, both, table, groups, band)
    spectral = physical_stage(slope_bands, axial, both, table, groups, band)
    shape = (3, part_count, slots, planes, modes)
    return radial_analysis(exchange(spectral), lens, back, analysis, shape)


def solution(mesh):
    placed = (P(None, None, "order", "axial", None), P(), P())
    return jax.shard_map(
        shards,
        mesh=mesh,
        in_specs=placed,
        out_specs=P(None, None, "order", "axial", None),
        check_vma=False,
    )
```

```python
import functools
import math

import jax
import jax.numpy as jnp
import numpy as np
from jax import lax
from jax.experimental import pallas as pl
from jax.experimental.pallas import tpu as pltpu
from jax.sharding import PartitionSpec as P

R = 1024
F32 = jnp.float32
BF16 = jnp.bfloat16


def radial_constants(radius_count, mode_count):
    radius_ids = np.arange(radius_count)
    mode_ids = np.arange(mode_count)
    phases = mode_ids[None, :] * (2 * radius_ids[:, None] + 1) % (4 * radius_count)
    cosines = np.cos(phases * (math.pi / (2 * radius_count))).astype(np.float32)
    synthesis = cosines.astype(jnp.bfloat16)
    analysis = (cosines * np.float32(math.sqrt(2.0 / radius_count))).astype(jnp.bfloat16)
    return synthesis, analysis


def plane_matrices(slots):
    width = 2 * slots * 2
    eye = np.eye(width // 2, dtype=np.float32)
    own = np.kron(eye, np.array([[0, 8], [-8, 0]], np.float32))
    low = np.kron(eye, np.array([[1, -8], [0, 1]], np.float32))
    high = np.kron(eye, np.array([[-1, 0], [8, -1]], np.float32))
    rows = np.concatenate([own, low, high], axis=1)
    per = 128 // slots
    source = np.arange(per * width).reshape(per, 2, slots, 2).transpose(3, 1, 0, 2).reshape(-1)
    permutation = np.zeros((per * width, per * width), np.float32)
    permutation[source, np.arange(per * width)] = 1.0
    return rows.astype(jnp.bfloat16), permutation.astype(jnp.bfloat16)


def dot(a, b, dims):
    return lax.dot_general(a, b, (dims, ((), ())), preferred_element_type=F32)


HERE = pl.BlockSpec(memory_space=pltpu.VMEM)
FAR = pl.BlockSpec(memory_space=pltpu.HBM)
SCALARS = pl.BlockSpec(memory_space=pltpu.SMEM)


def in_hbm(x):
    return pltpu.with_memory_space_constraint(x, pltpu.HBM)


def call(kernel, name, out_shape, in_specs, out_specs, scratch=(), limit=16):
    return pl.pallas_call(
        kernel,
        out_shape=out_shape,
        in_specs=in_specs,
        out_specs=out_specs,
        scratch_shapes=list(scratch),
        compiler_params=pltpu.CompilerParams(vmem_limit_bytes=limit << 20),
        name=name,
    )


def stage_kernel(x_ref, out_ref, sem):
    fields, parts, slots = out_ref.shape[:3]
    copies = []
    for field in range(fields):
        for part in range(parts):
            for half in range(2):
                area = (field, part, pl.ds(half * (slots // 2), slots // 2))
                copies.append(pltpu.make_async_copy(
                    x_ref.at[area], out_ref.at[area], sem.at[len(copies)]))
                copies[-1].start()
    for copy in copies:
        copy.wait()


def stage(x):
    return call(
        stage_kernel, "stage", pltpu.VMEM((3,) + x.shape[1:], BF16),
        [FAR], HERE, [pltpu.SemaphoreType.DMA((12,))],
    )(in_hbm(x))


def field_rows(ref, field):
    block = ref[field]
    return block.reshape(math.prod(block.shape[:-1]), block.shape[-1])


def masked_rows(block, lens, weight):
    modes = lax.broadcasted_iota(jnp.int32, block.shape, 1)
    return jnp.where(modes < lens[:, :1], block.astype(F32) * weight[:, :1], 0.0).astype(BF16)


def send_bands(table_ref, rows, out_ref, buffer, sem, loads=None, count=4):
    size = table_ref.shape[0] // count
    copies = []
    for i in range(count):
        part = pl.ds(i * size, size)
        if loads is not None:
            loads[i].wait()
        buffer[part, :] = dot(table_ref[part, :], rows, ((1,), (1,))).astype(BF16)
        copies.append(pltpu.make_async_copy(buffer.at[part], out_ref.at[part], sem.at[i]))
        copies[-1].start()
    for copy in copies:
        copy.wait()


def slot_rows(orders, lengths, slots):
    index = lax.axis_index("order")
    per_row = 128 // slots
    lane = lax.broadcasted_iota(jnp.int32, (128, 128), 1)
    held = jnp.broadcast_to(orders[pl.ds(index // per_row, 1), :], (128, 128)).T
    total = jnp.zeros((128, 128), F32)
    for row in range(lengths.shape[0]):
        wide = jnp.broadcast_to(lengths[row:row + 1, :], (128, 128)).astype(F32)
        total += jnp.where(held == lane + row * 128, wide, 0.0)
    found = jnp.sum(total, axis=1, keepdims=True).astype(jnp.int32)
    found = jnp.broadcast_to(found, (128, 128))
    zero = jnp.where(held == 0, 1, 0)
    columns = jnp.where(lane == 0, found >> 3, jnp.where(lane == 1, found & 7, zero))
    rows = lax.broadcasted_iota(jnp.int32, (2 * slots, 128), 0) // 2
    picked = lax.broadcasted_iota(jnp.int32, (2 * slots, 128), 1)
    pick = jnp.where(picked == rows + (index % per_row) * slots, 1.0, 0.0).astype(BF16)
    result = dot(pick, columns.astype(F32).astype(BF16), ((1,), (0,)))
    lens = (result[:, 0:1] * 8.0 + result[:, 1:2]).astype(jnp.int32)
    weight = 2.0 - result[:, 2:3]
    return jnp.concatenate([lens, lens], axis=0), jnp.concatenate([weight, weight], axis=0)


def raw_kernel(orders_far, lengths_far, x_far, table_far, out_ref, lens_ref, weight_ref,
               buffer, sem, orders, lengths, x_ref, small_sem, table, load_sem):
    size = table.shape[0] // 4
    small = [
        pltpu.make_async_copy(orders_far, orders, small_sem.at[0]),
        pltpu.make_async_copy(lengths_far, lengths, small_sem.at[1]),
        pltpu.make_async_copy(x_far.at[3, 0], x_ref.at[0], small_sem.at[2]),
        pltpu.make_async_copy(x_far.at[3, 1], x_ref.at[1], small_sem.at[3]),
    ]
    loads = [
        pltpu.make_async_copy(table_far.at[pl.ds(i * size, size)],
                              table.at[pl.ds(i * size, size)], load_sem.at[i])
        for i in range(4)
    ]
    for copy in small + loads:
        copy.start()
    small[0].wait()
    small[1].wait()
    lens, weight = slot_rows(orders, lengths, x_ref.shape[1])
    lens_ref[...] = jnp.broadcast_to(lens, lens_ref.shape)
    weight_ref[...] = jnp.broadcast_to(weight, weight_ref.shape)
    small[2].wait()
    small[3].wait()
    block = x_ref[...]
    block = block.reshape(math.prod(block.shape[:-1]), block.shape[-1])
    send_bands(table, masked_rows(block, lens, weight), out_ref, buffer, sem, loads)


def radial_raw(orders, lengths, x, table):
    rows = math.prod(x.shape[1:-1])
    return call(
        raw_kernel, "radial_raw",
        (pltpu.HBM((R, rows), BF16),
         jax.ShapeDtypeStruct((rows, 128), jnp.int32),
         jax.ShapeDtypeStruct((rows, 128), F32)),
        [FAR] * 4, (FAR, HERE, HERE),
        [pltpu.VMEM((R, rows), BF16), pltpu.SemaphoreType.DMA((4,)),
         pltpu.VMEM(orders.shape, jnp.int32), pltpu.VMEM(lengths.shape, jnp.int32),
         pltpu.VMEM(x.shape[1:], BF16), pltpu.SemaphoreType.DMA((4,)),
         pltpu.VMEM(table.shape, BF16), pltpu.SemaphoreType.DMA((4,))],
    )(in_hbm(orders), in_hbm(lengths), in_hbm(x), in_hbm(table))


def slope_kernel(x_ref, low_ref, high_ref, lens_ref, weight_ref, rows_ref, table_ref, out_ref,
                 buffer, sem):
    held = []
    for field in range(3):
        stacked = jnp.concatenate(
            [field_rows(x_ref, field), field_rows(low_ref, field), field_rows(high_ref, field)],
            axis=0,
        )
        slope = dot(rows_ref[...], stacked, ((1,), (0,)))
        held.append(masked_rows(slope, lens_ref[...], weight_ref[...]))
    send_bands(table_ref, jnp.concatenate(held, axis=0), out_ref, buffer, sem)


def radial_slope(x, low, high, lens, weight, rows_map, table):
    rows = math.prod(x.shape[:-1])
    return call(
        slope_kernel, "radial_slope", pltpu.HBM((R, rows), BF16), [HERE] * 7, FAR,
        [pltpu.VMEM((R, rows), BF16), pltpu.SemaphoreType.DMA((4,))],
    )(x, low, high, lens, weight, rows_map, table)


def sine_cosine(phase, points):
    centred = ((phase + points // 2) & (points - 1)) - points // 2
    y = centred.astype(F32) * (math.pi / points)
    square = y * y
    sine = jnp.float32(0.0)
    for n in (11, 9, 7, 5, 3, 1):
        sine = sine * square + (-1.0) ** (n // 2) / math.factorial(n)
    sine = sine * y
    cosine = jnp.float32(0.0)
    for n in (12, 10, 8, 6, 4, 2, 0):
        cosine = cosine * square + (-1.0) ** (n // 2) / math.factorial(n)
    return 1.0 - 2.0 * sine * sine, 2.0 * sine * cosine


def table_kernel(slots, orders_ref, far_ref, out_ref, sem):
    half = 128 * orders_ref.shape[0]
    points = 2 * half
    lane = lax.broadcasted_iota(jnp.int32, (slots, 128), 1)
    copies = []
    for row in range(orders_ref.shape[0]):
        column = jnp.broadcast_to(orders_ref[row:row + 1, :], (128, 128)).T
        for piece in range(128 // slots):
            orders = column[piece * slots:(piece + 1) * slots]
            rows = pl.ds(row * 128 + piece * slots, slots)
            cos_now, sin_now = sine_cosine((orders * lane) & (points - 1), points)
            cos_turn, sin_turn = sine_cosine((orders * 128) & (points - 1), points)
            for block in range(half // 128):
                out_ref[rows, pl.ds(block * 128, 128)] = cos_now.astype(BF16)
                out_ref[rows, pl.ds(half + (block + 1) * 128, 128)] = (-sin_now).astype(BF16)
                cos_now, sin_now = (
                    cos_now * cos_turn - sin_now * sin_turn,
                    sin_now * cos_turn + cos_now * sin_turn,
                )
            sign = jnp.where(lane == 0, 1 - 2 * (orders & 1), 0)
            out_ref[rows, pl.ds(half, 128)] = sign.astype(F32).astype(BF16)
        part = pl.ds(row * 128, 128)
        copies.append(pltpu.make_async_copy(out_ref.at[part], far_ref.at[part], sem.at[row]))
        copies[-1].start()
    for copy in copies:
        copy.wait()


def azimuthal_table(orders, slots):
    shape = (orders.size, 2 * orders.size + 128)
    return call(
        functools.partial(table_kernel, slots), "azimuthal_table",
        pltpu.HBM(shape, BF16), [HERE], FAR,
        [pltpu.VMEM(shape, BF16), pltpu.SemaphoreType.DMA((orders.shape[0],))],
    )(orders)


def place_field(lhs, row, bands, perm_ref, groups, band):
    per = perm_ref.shape[0] // bands.shape[1]
    stacked = jnp.concatenate([
        jnp.concatenate(
            [bands[(tile * per + e) * band:(tile * per + e + 1) * band] for e in range(per)], axis=1
        )
        for tile in range(groups // per)
    ], axis=0)
    mapped = dot(stacked, perm_ref[...], ((1,), (0,))).astype(BF16)
    for tile in range(groups // per):
        for plane in range(2):
            for part in range(2):
                lanes = (2 * plane + part) * 128
                lhs[part, row + plane * band:row + (plane + 1) * band,
                    pl.ds(tile * 128, 128)] = mapped[tile * band:(tile + 1) * band,
                                                     lanes:lanes + 128]


def table_loads(far_ref, table_ref, sem):
    rows, columns = table_ref.shape
    half = rows
    step = half // 2
    pieces = [(0, step), (half + 128, step), (step, step + 128), (half + 128 + step, step)]
    loads = []
    for start, size in pieces:
        loads.append([])
        for piece in range(4):
            area = (pl.ds(piece * (rows // 4), rows // 4), pl.ds(start, size))
            index = 4 * (len(loads) - 1) + piece
            loads[-1].append(pltpu.make_async_copy(
                far_ref.at[area], table_ref.at[area], sem.at[index]))
            loads[-1][-1].start()
    return pieces, loads


def axial_kernel(groups, band, raw_ref, perm_ref, far_ref, axial_ref, lhs, table_ref, sem):
    pieces, loads = table_loads(far_ref, table_ref, sem)
    place_field(lhs, 0, raw_ref[...], perm_ref, groups, band)
    half = table_ref.shape[0]
    for index, (start, size) in enumerate(pieces):
        for load in loads[index]:
            load.wait()
        part = pl.ds(start, size)
        values = dot(lhs[index % 2], table_ref[:, part], ((1,), (0,)))
        column = lax.broadcasted_iota(jnp.int32, values.shape, 1) + start
        once = (column == 0) | (column == half)
        axial_ref[:, part] = values * jnp.where(once, 1.0 / 12.0, 1.0 / 6.0)


def axial_stage(raw, perm, table, groups, band):
    rows, columns = table.shape
    return call(
        functools.partial(axial_kernel, groups, band), "axial_stage",
        jax.ShapeDtypeStruct((2 * band, columns), F32),
        [HERE, HERE, FAR], HERE,
        [pltpu.VMEM((2, 2 * band, rows), BF16), pltpu.VMEM(table.shape, BF16),
         pltpu.SemaphoreType.DMA((16,))],
    )(raw, perm, in_hbm(table))


def physical_kernel(groups, band, step, scale, slope_ref, axial_ref, perm_ref, far_ref, out_ref,
                    lhs, even, odd, table_ref, sem):
    pieces, loads = table_loads(far_ref, table_ref, sem)
    width = slope_ref.shape[1] // 3
    half = table_ref.shape[0]
    per = perm_ref.shape[0] // width
    for field in range(3):
        place_field(lhs, 2 * field * band, slope_ref[:, field * width:(field + 1) * width],
                    perm_ref, groups, band)
    for index in (0, 2):
        (start, size), (other, span) = pieces[index], pieces[index + 1]
        for load in loads[index]:
            load.wait()
        cosines = dot(lhs[0], table_ref[:, pl.ds(start, size)], ((1,), (0,)))
        for load in loads[index + 1]:
            load.wait()
        sines = dot(lhs[1], table_ref[:, pl.ds(other, span)], ((1,), (0,)))
        axial_cos = axial_ref[:, pl.ds(start, size)]
        axial_sin = axial_ref[:, pl.ds(other, span)]
        for g in range(3):
            area = slice(2 * g * band, (2 * g + 2) * band)
            c, s = cosines[area], sines[area]
            part = pl.ds(start, span)
            even[area, part] = (c[:, :span] * axial_cos[:, :span] + s * axial_sin).astype(BF16)
            odd[area, part] = (c[:, :span] * axial_sin + s * axial_cos[:, :span]).astype(BF16)
            if size > span:
                edge = (c[:, span:] * axial_cos[:, span:]).astype(BF16)
                even[area, pl.ds(start + span, size - span)] = edge

    for start in range(0, half, step):
        rows = pl.ds(start, step)
        parts = [
            (dot(even[...], table_ref[rows, 0:half + 128], ((1,), (1,))) * scale).astype(BF16),
            (dot(odd[...], table_ref[rows, half + 128:], ((1,), (1,))) * scale).astype(BF16),
        ]
        stacked = jnp.concatenate([
            jnp.concatenate([
                parts[part][(2 * g + plane) * band:(2 * g + plane + 1) * band,
                            tile * 128:(tile + 1) * 128]
                for plane in range(2) for part in range(2)
            ], axis=1)
            for g in range(3) for tile in range(step // 128)
        ], axis=0)
        mapped = dot(stacked, perm_ref[...], ((1,), (1,))).astype(BF16)
        for g in range(3):
            for tile in range(step // 128):
                source = (g * (step // 128) + tile) * band
                for e in range(per):
                    row = ((start // 128 + tile) * per + e) * band
                    out_ref[row:row + band, pl.ds(g * width, width)] = mapped[
                        source:source + band, e * width:(e + 1) * width]


def physical_stage(slope, axial, perm, table, groups, band, step=512):
    rows = table.shape[0]
    scale = math.sqrt(1.0 / rows)
    return call(
        functools.partial(physical_kernel, groups, band, step, scale), "physical_stage",
        jax.ShapeDtypeStruct(slope.shape, BF16), [HERE] * 3 + [FAR], HERE,
        [pltpu.VMEM((2, 6 * band, rows), BF16), pltpu.VMEM((6 * band, rows + 128), BF16),
         pltpu.VMEM((6 * band, rows), BF16), pltpu.VMEM(table.shape, BF16),
         pltpu.SemaphoreType.DMA((16,))],
        limit=28,
    )(slope, axial, perm, in_hbm(table))


def final_kernel(x_ref, lens_ref, table_ref, out_ref, buffer, sem):
    width = x_ref.shape[1] // 3
    modes = lax.broadcasted_iota(jnp.int32, (width, table_ref.shape[1]), 1)
    keep = modes < lens_ref[:, :1]
    copies = []
    for g in range(3):
        part = x_ref[:, g * width:(g + 1) * width]
        result = dot(part, table_ref[...], ((0,), (0,)))
        rows = jnp.where(keep, result, 0.0).astype(BF16)
        buffer[g] = rows.reshape(buffer.shape[1:])
        copies.append(pltpu.make_async_copy(buffer.at[g], out_ref.at[g], sem.at[g]))
        copies[-1].start()
    for copy in copies:
        copy.wait()


def radial_analysis(x, lens, table, shape):
    return call(
        final_kernel, "radial_analysis", pltpu.HBM(shape, BF16), [HERE] * 3, FAR,
        [pltpu.VMEM(shape, BF16), pltpu.SemaphoreType.DMA((3,))],
    )(x, lens, table)


def shift(block, offset):
    count = lax.axis_size("axial")
    return lax.ppermute(block, "axial", [(i, (i + offset) % count) for i in range(count)])


def exchange(block):
    return lax.all_to_all(block, "order", split_axis=0, concat_axis=0, tiled=True)


def shards(coefficients, order_lists, lengths):
    field_count, part_count, slots, planes, modes = coefficients.shape
    order_count = order_lists.shape[0]
    groups = lax.axis_size("order")
    band = R // groups
    width = part_count * slots * planes
    synthesis, analysis = radial_constants(R, modes)
    rows_map, perm = plane_matrices(slots)

    sloped = stage(coefficients)
    low, high = shift(sloped, 1), shift(sloped, -1)
    orders = order_lists.reshape(order_count // 128, 128)
    bands, lens, weight = radial_raw(
        orders, lengths.reshape(order_count // 128, 128), coefficients, synthesis
    )
    raw_bands = exchange(bands)
    table = azimuthal_table(orders, slots)
    later_lens, table = lax.optimization_barrier((lens, table))
    slope_bands = exchange(
        radial_slope(sloped, low, high, later_lens, weight, rows_map, synthesis)
    )
    axial = axial_stage(raw_bands, perm, table, groups, band)
    spectral = physical_stage(slope_bands, axial, perm, table, groups, band)
    shape = (3, part_count, slots, planes, modes)
    return radial_analysis(exchange(spectral), lens, analysis, shape)


def solution(mesh):
    placed = (P(None, None, "order", "axial", None), P(), P())
    return jax.shard_map(
        shards,
        mesh=mesh,
        in_specs=placed,
        out_specs=P(None, None, "order", "axial", None),
        check_vma=False,
    )
```

```python
import functools
import math

import jax
import jax.numpy as jnp
import numpy as np
from jax import lax
from jax.experimental import pallas as pl
from jax.experimental.pallas import tpu as pltpu
from jax.sharding import PartitionSpec as P

R = 1024
F32 = jnp.float32
BF16 = jnp.bfloat16


def radial_constants(radius_count, mode_count):
    radius_ids = np.arange(radius_count)
    mode_ids = np.arange(mode_count)
    phases = mode_ids[None, :] * (2 * radius_ids[:, None] + 1) % (4 * radius_count)
    cosines = np.cos(phases * (math.pi / (2 * radius_count))).astype(np.float32)
    synthesis = cosines.astype(jnp.bfloat16)
    analysis = (cosines * np.float32(math.sqrt(2.0 / radius_count))).astype(jnp.bfloat16)
    return synthesis, analysis


def plane_matrices(slots):
    width = 2 * slots * 2
    eye = np.eye(width // 2, dtype=np.float32)
    own = np.kron(eye, np.array([[0, 8], [-8, 0]], np.float32))
    low = np.kron(eye, np.array([[1, -8], [0, 1]], np.float32))
    high = np.kron(eye, np.array([[-1, 0], [8, -1]], np.float32))
    rows = np.concatenate([own, low, high], axis=1)
    per = 128 // slots
    source = np.arange(per * width).reshape(per, 2, slots, 2).transpose(3, 1, 0, 2).reshape(-1)
    permutation = np.zeros((per * width, per * width), np.float32)
    permutation[source, np.arange(per * width)] = 1.0
    return rows.astype(jnp.bfloat16), permutation.astype(jnp.bfloat16)


def dot(a, b, dims):
    return lax.dot_general(a, b, (dims, ((), ())), preferred_element_type=F32)


HERE = pl.BlockSpec(memory_space=pltpu.VMEM)
FAR = pl.BlockSpec(memory_space=pltpu.HBM)
SCALARS = pl.BlockSpec(memory_space=pltpu.SMEM)


def in_hbm(x):
    return pltpu.with_memory_space_constraint(x, pltpu.HBM)


def call(kernel, name, out_shape, in_specs, out_specs, scratch=(), limit=16):
    return pl.pallas_call(
        kernel,
        out_shape=out_shape,
        in_specs=in_specs,
        out_specs=out_specs,
        scratch_shapes=list(scratch),
        compiler_params=pltpu.CompilerParams(vmem_limit_bytes=limit << 20),
        name=name,
    )


def stage_kernel(x_ref, out_ref, held, sem):
    fields, parts, slots = held.shape[:3]
    copies = []
    for field in range(fields):
        for part in range(parts):
            for half in range(2):
                area = (field, part, pl.ds(half * (slots // 2), slots // 2))
                copies.append(pltpu.make_async_copy(
                    x_ref.at[area], held.at[area], sem.at[len(copies)]))
                copies[-1].start()
    rows = out_ref.shape[0] // fields
    for field in range(fields):
        for copy in copies[4 * field:4 * field + 4]:
            copy.wait()
        out_ref[field * rows:(field + 1) * rows, :] = held[field].reshape(rows, held.shape[-1])


def stage(x):
    rows, modes = 3 * math.prod(x.shape[1:-1]), x.shape[-1]
    return call(
        stage_kernel, "stage", pltpu.VMEM((rows, modes), BF16),
        [FAR], HERE, [pltpu.VMEM((3,) + x.shape[1:], BF16), pltpu.SemaphoreType.DMA((12,))],
    )(in_hbm(x))


def masked_rows(block, lens, weight):
    modes = lax.broadcasted_iota(jnp.int32, block.shape, 1)
    return jnp.where(modes < lens[:, :1], block.astype(F32) * weight[:, :1], 0.0).astype(BF16)


def send_bands(table_ref, rows, out_ref, buffer, sem, loads=None, count=4):
    size = table_ref.shape[0] // count
    copies = []
    for i in range(count):
        part = pl.ds(i * size, size)
        if loads is not None:
            loads[i].wait()
        buffer[part, :] = dot(table_ref[part, :], rows, ((1,), (1,))).astype(BF16)
        copies.append(pltpu.make_async_copy(buffer.at[part], out_ref.at[part], sem.at[i]))
        copies[-1].start()
    for copy in copies:
        copy.wait()


def slot_rows(orders, lengths, slots):
    index = lax.axis_index("order")
    per_row = 128 // slots
    lane = lax.broadcasted_iota(jnp.int32, (128, 128), 1)
    held = jnp.broadcast_to(orders[pl.ds(index // per_row, 1), :], (128, 128)).T
    total = jnp.zeros((128, 128), F32)
    for row in range(lengths.shape[0]):
        wide = jnp.broadcast_to(lengths[row:row + 1, :], (128, 128)).astype(F32)
        total += jnp.where(held == lane + row * 128, wide, 0.0)
    found = jnp.sum(total, axis=1, keepdims=True).astype(jnp.int32)
    found = jnp.broadcast_to(found, (128, 128))
    zero = jnp.where(held == 0, 1, 0)
    columns = jnp.where(lane == 0, found >> 3, jnp.where(lane == 1, found & 7, zero))
    rows = lax.broadcasted_iota(jnp.int32, (2 * slots, 128), 0) // 2
    picked = lax.broadcasted_iota(jnp.int32, (2 * slots, 128), 1)
    pick = jnp.where(picked == rows + (index % per_row) * slots, 1.0, 0.0).astype(BF16)
    result = dot(pick, columns.astype(F32).astype(BF16), ((1,), (0,)))
    lens = (result[:, 0:1] * 8.0 + result[:, 1:2]).astype(jnp.int32)
    weight = 2.0 - result[:, 2:3]
    return jnp.concatenate([lens, lens], axis=0), jnp.concatenate([weight, weight], axis=0)


def raw_kernel(orders_far, lengths_far, x_far, table_far, out_ref, lens_ref, weight_ref,
               buffer, sem, orders, lengths, x_ref, small_sem, table, load_sem):
    size = table.shape[0] // 4
    small = [
        pltpu.make_async_copy(orders_far, orders, small_sem.at[0]),
        pltpu.make_async_copy(lengths_far, lengths, small_sem.at[1]),
        pltpu.make_async_copy(x_far.at[3, 0], x_ref.at[0], small_sem.at[2]),
        pltpu.make_async_copy(x_far.at[3, 1], x_ref.at[1], small_sem.at[3]),
    ]
    loads = [
        pltpu.make_async_copy(table_far.at[pl.ds(i * size, size)],
                              table.at[pl.ds(i * size, size)], load_sem.at[i])
        for i in range(4)
    ]
    for copy in small + loads:
        copy.start()
    small[0].wait()
    small[1].wait()
    lens, weight = slot_rows(orders, lengths, x_ref.shape[1])
    lens_ref[...] = jnp.broadcast_to(lens, lens_ref.shape)
    weight_ref[...] = jnp.broadcast_to(weight, weight_ref.shape)
    small[2].wait()
    small[3].wait()
    block = x_ref[...]
    block = block.reshape(math.prod(block.shape[:-1]), block.shape[-1])
    send_bands(table, masked_rows(block, lens, weight), out_ref, buffer, sem, loads)


def radial_raw(orders, lengths, x, table):
    rows = math.prod(x.shape[1:-1])
    return call(
        raw_kernel, "radial_raw",
        (pltpu.HBM((R, rows), BF16),
         jax.ShapeDtypeStruct((rows, 128), jnp.int32),
         jax.ShapeDtypeStruct((rows, 128), F32)),
        [FAR] * 4, (FAR, HERE, HERE),
        [pltpu.VMEM((R, rows), BF16), pltpu.SemaphoreType.DMA((4,)),
         pltpu.VMEM(orders.shape, jnp.int32), pltpu.VMEM(lengths.shape, jnp.int32),
         pltpu.VMEM(x.shape[1:], BF16), pltpu.SemaphoreType.DMA((4,)),
         pltpu.VMEM(table.shape, BF16), pltpu.SemaphoreType.DMA((4,))],
    )(in_hbm(orders), in_hbm(lengths), in_hbm(x), in_hbm(table))


def slope_kernel(x_ref, low_ref, high_ref, lens_ref, weight_ref, rows_ref, table_ref, out_ref,
                 buffer, sem):
    held = []
    count = x_ref.shape[0] // 3
    for field in range(3):
        rows = pl.ds(field * count, count)
        stacked = jnp.concatenate([x_ref[rows, :], low_ref[rows, :], high_ref[rows, :]], axis=0)
        slope = dot(rows_ref[...], stacked, ((1,), (0,)))
        held.append(masked_rows(slope, lens_ref[...], weight_ref[...]))
    send_bands(table_ref, jnp.concatenate(held, axis=0), out_ref, buffer, sem)


def radial_slope(x, low, high, lens, weight, rows_map, table):
    rows = x.shape[0]
    return call(
        slope_kernel, "radial_slope", pltpu.HBM((R, rows), BF16), [HERE] * 7, FAR,
        [pltpu.VMEM((R, rows), BF16), pltpu.SemaphoreType.DMA((4,))],
    )(x, low, high, lens, weight, rows_map, table)


def sine_cosine(phase, points):
    centred = ((phase + points // 2) & (points - 1)) - points // 2
    y = centred.astype(F32) * (math.pi / points)
    square = y * y
    sine = jnp.float32(0.0)
    for n in (11, 9, 7, 5, 3, 1):
        sine = sine * square + (-1.0) ** (n // 2) / math.factorial(n)
    sine = sine * y
    cosine = jnp.float32(0.0)
    for n in (12, 10, 8, 6, 4, 2, 0):
        cosine = cosine * square + (-1.0) ** (n // 2) / math.factorial(n)
    return 1.0 - 2.0 * sine * sine, 2.0 * sine * cosine


def table_kernel(slots, orders_ref, far_ref, out_ref, sem):
    half = 128 * orders_ref.shape[0]
    points = 2 * half
    lane = lax.broadcasted_iota(jnp.int32, (slots, 128), 1)
    copies = []
    for row in range(orders_ref.shape[0]):
        column = jnp.broadcast_to(orders_ref[row:row + 1, :], (128, 128)).T
        for piece in range(128 // slots):
            orders = column[piece * slots:(piece + 1) * slots]
            rows = pl.ds(row * 128 + piece * slots, slots)
            cos_now, sin_now = sine_cosine((orders * lane) & (points - 1), points)
            cos_turn, sin_turn = sine_cosine((orders * 128) & (points - 1), points)
            for block in range(half // 128):
                out_ref[rows, pl.ds(block * 128, 128)] = cos_now.astype(BF16)
                out_ref[rows, pl.ds(half + (block + 1) * 128, 128)] = (-sin_now).astype(BF16)
                cos_now, sin_now = (
                    cos_now * cos_turn - sin_now * sin_turn,
                    sin_now * cos_turn + cos_now * sin_turn,
                )
            sign = jnp.where(lane == 0, 1 - 2 * (orders & 1), 0)
            out_ref[rows, pl.ds(half, 128)] = sign.astype(F32).astype(BF16)
        part = pl.ds(row * 128, 128)
        copies.append(pltpu.make_async_copy(out_ref.at[part], far_ref.at[part], sem.at[row]))
        copies[-1].start()
    for copy in copies:
        copy.wait()


def azimuthal_table(orders, slots):
    shape = (orders.size, 2 * orders.size + 128)
    return call(
        functools.partial(table_kernel, slots), "azimuthal_table",
        pltpu.HBM(shape, BF16), [HERE], FAR,
        [pltpu.VMEM(shape, BF16), pltpu.SemaphoreType.DMA((orders.shape[0],))],
    )(orders)


def place_field(lhs, row, bands, perm_ref, groups, band):
    per = perm_ref.shape[0] // bands.shape[1]
    stacked = jnp.concatenate([
        jnp.concatenate(
            [bands[(tile * per + e) * band:(tile * per + e + 1) * band] for e in range(per)], axis=1
        )
        for tile in range(groups // per)
    ], axis=0)
    mapped = dot(stacked, perm_ref[...], ((1,), (0,))).astype(BF16)
    for tile in range(groups // per):
        for plane in range(2):
            for part in range(2):
                lanes = (2 * plane + part) * 128
                lhs[part, row + plane * band:row + (plane + 1) * band,
                    pl.ds(tile * 128, 128)] = mapped[tile * band:(tile + 1) * band,
                                                     lanes:lanes + 128]


def table_loads(far_ref, table_ref, sem):
    rows, columns = table_ref.shape
    half = rows
    step = half // 2
    pieces = [(0, step), (half + 128, step), (step, step + 128), (half + 128 + step, step)]
    loads = []
    for start, size in pieces:
        loads.append([])
        for piece in range(4):
            area = (pl.ds(piece * (rows // 4), rows // 4), pl.ds(start, size))
            index = 4 * (len(loads) - 1) + piece
            loads[-1].append(pltpu.make_async_copy(
                far_ref.at[area], table_ref.at[area], sem.at[index]))
            loads[-1][-1].start()
    return pieces, loads


def axial_kernel(groups, band, raw_ref, perm_ref, far_ref, axial_ref, lhs, table_ref, sem):
    pieces, loads = table_loads(far_ref, table_ref, sem)
    place_field(lhs, 0, raw_ref[...], perm_ref, groups, band)
    half = table_ref.shape[0]
    for index, (start, size) in enumerate(pieces):
        for load in loads[index]:
            load.wait()
        part = pl.ds(start, size)
        values = dot(lhs[index % 2], table_ref[:, part], ((1,), (0,)))
        column = lax.broadcasted_iota(jnp.int32, values.shape, 1) + start
        once = (column == 0) | (column == half)
        axial_ref[:, part] = values * jnp.where(once, 1.0 / 12.0, 1.0 / 6.0)


def axial_stage(raw, perm, table, groups, band):
    rows, columns = table.shape
    return call(
        functools.partial(axial_kernel, groups, band), "axial_stage",
        jax.ShapeDtypeStruct((2 * band, columns), F32),
        [HERE, HERE, FAR], HERE,
        [pltpu.VMEM((2, 2 * band, rows), BF16), pltpu.VMEM(table.shape, BF16),
         pltpu.SemaphoreType.DMA((16,))],
    )(raw, perm, in_hbm(table))


def physical_kernel(groups, band, step, scale, slope_ref, axial_ref, perm_ref, far_ref, out_ref,
                    lhs, even, odd, table_ref, sem):
    pieces, loads = table_loads(far_ref, table_ref, sem)
    width = slope_ref.shape[1] // 3
    half = table_ref.shape[0]
    per = perm_ref.shape[0] // width
    for field in range(3):
        place_field(lhs, 2 * field * band, slope_ref[:, field * width:(field + 1) * width],
                    perm_ref, groups, band)
    for index in (0, 2):
        (start, size), (other, span) = pieces[index], pieces[index + 1]
        for load in loads[index]:
            load.wait()
        cosines = dot(lhs[0], table_ref[:, pl.ds(start, size)], ((1,), (0,)))
        for load in loads[index + 1]:
            load.wait()
        sines = dot(lhs[1], table_ref[:, pl.ds(other, span)], ((1,), (0,)))
        axial_cos = axial_ref[:, pl.ds(start, size)]
        axial_sin = axial_ref[:, pl.ds(other, span)]
        for g in range(3):
            area = slice(2 * g * band, (2 * g + 2) * band)
            c, s = cosines[area], sines[area]
            part = pl.ds(start, span)
            even[area, part] = (c[:, :span] * axial_cos[:, :span] + s * axial_sin).astype(BF16)
            odd[area, part] = (c[:, :span] * axial_sin + s * axial_cos[:, :span]).astype(BF16)
            if size > span:
                edge = (c[:, span:] * axial_cos[:, span:]).astype(BF16)
                even[area, pl.ds(start + span, size - span)] = edge

    for start in range(0, half, step):
        rows = pl.ds(start, step)
        parts = [
            (dot(even[...], table_ref[rows, 0:half + 128], ((1,), (1,))) * scale).astype(BF16),
            (dot(odd[...], table_ref[rows, half + 128:], ((1,), (1,))) * scale).astype(BF16),
        ]
        stacked = jnp.concatenate([
            jnp.concatenate([
                parts[part][(2 * g + plane) * band:(2 * g + plane + 1) * band,
                            tile * 128:(tile + 1) * 128]
                for plane in range(2) for part in range(2)
            ], axis=1)
            for g in range(3) for tile in range(step // 128)
        ], axis=0)
        mapped = dot(stacked, perm_ref[...], ((1,), (1,))).astype(BF16)
        for g in range(3):
            for tile in range(step // 128):
                source = (g * (step // 128) + tile) * band
                for e in range(per):
                    row = ((start // 128 + tile) * per + e) * band
                    out_ref[row:row + band, pl.ds(g * width, width)] = mapped[
                        source:source + band, e * width:(e + 1) * width]


def physical_stage(slope, axial, perm, table, groups, band, step=512):
    rows = table.shape[0]
    scale = math.sqrt(1.0 / rows)
    return call(
        functools.partial(physical_kernel, groups, band, step, scale), "physical_stage",
        jax.ShapeDtypeStruct(slope.shape, BF16), [HERE] * 3 + [FAR], HERE,
        [pltpu.VMEM((2, 6 * band, rows), BF16), pltpu.VMEM((6 * band, rows + 128), BF16),
         pltpu.VMEM((6 * band, rows), BF16), pltpu.VMEM(table.shape, BF16),
         pltpu.SemaphoreType.DMA((16,))],
        limit=28,
    )(slope, axial, perm, in_hbm(table))


def final_kernel(x_ref, lens_ref, table_ref, out_ref, buffer, sem):
    width = x_ref.shape[1] // 3
    modes = lax.broadcasted_iota(jnp.int32, (width, table_ref.shape[1]), 1)
    keep = modes < lens_ref[:, :1]
    copies = []
    for g in range(3):
        part = x_ref[:, g * width:(g + 1) * width]
        result = dot(part, table_ref[...], ((0,), (0,)))
        rows = jnp.where(keep, result, 0.0).astype(BF16)
        buffer[g] = rows.reshape(buffer.shape[1:])
        copies.append(pltpu.make_async_copy(buffer.at[g], out_ref.at[g], sem.at[g]))
        copies[-1].start()
    for copy in copies:
        copy.wait()


def radial_analysis(x, lens, table, shape):
    return call(
        final_kernel, "radial_analysis", pltpu.HBM(shape, BF16), [HERE] * 3, FAR,
        [pltpu.VMEM(shape, BF16), pltpu.SemaphoreType.DMA((3,))],
    )(x, lens, table)


def shift(block, offset):
    count = lax.axis_size("axial")
    return lax.ppermute(block, "axial", [(i, (i + offset) % count) for i in range(count)])


def exchange(block):
    return lax.all_to_all(block, "order", split_axis=0, concat_axis=0, tiled=True)


def shards(coefficients, order_lists, lengths):
    field_count, part_count, slots, planes, modes = coefficients.shape
    order_count = order_lists.shape[0]
    groups = lax.axis_size("order")
    band = R // groups
    width = part_count * slots * planes
    synthesis, analysis = radial_constants(R, modes)
    rows_map, perm = plane_matrices(slots)

    sloped = stage(coefficients)
    low, high = shift(sloped, 1), shift(sloped, -1)
    orders = order_lists.reshape(order_count // 128, 128)
    bands, lens, weight = radial_raw(
        orders, lengths.reshape(order_count // 128, 128), coefficients, synthesis
    )
    raw_bands = exchange(bands)
    table = azimuthal_table(orders, slots)
    slope_bands = exchange(
        radial_slope(sloped, low, high, lens, weight, rows_map, synthesis)
    )
    axial = axial_stage(raw_bands, perm, table, groups, band)
    spectral = physical_stage(slope_bands, axial, perm, table, groups, band)
    shape = (3, part_count, slots, planes, modes)
    return radial_analysis(exchange(spectral), lens, analysis, shape)


def solution(mesh):
    placed = (P(None, None, "order", "axial", None), P(), P())
    return jax.shard_map(
        shards,
        mesh=mesh,
        in_specs=placed,
        out_specs=P(None, None, "order", "axial", None),
        check_vma=False,
    )
```

```python
import functools
import math

import jax
import jax.numpy as jnp
import numpy as np
from jax import lax
from jax.experimental import pallas as pl
from jax.experimental.pallas import tpu as pltpu
from jax.sharding import PartitionSpec as P

R = 1024
F32 = jnp.float32
BF16 = jnp.bfloat16


def radial_constants(radius_count, mode_count):
    radius_ids = np.arange(radius_count)
    mode_ids = np.arange(mode_count)
    phases = mode_ids[None, :] * (2 * radius_ids[:, None] + 1) % (4 * radius_count)
    cosines = np.cos(phases * (math.pi / (2 * radius_count))).astype(np.float32)
    synthesis = cosines.astype(jnp.bfloat16)
    analysis = (cosines * np.float32(math.sqrt(2.0 / radius_count))).astype(jnp.bfloat16)
    return synthesis, analysis


def plane_matrices(slots):
    width = 2 * slots * 2
    eye = np.eye(width // 2, dtype=np.float32)
    own = np.kron(eye, np.array([[0, 8], [-8, 0]], np.float32))
    low = np.kron(eye, np.array([[1, -8], [0, 1]], np.float32))
    high = np.kron(eye, np.array([[-1, 0], [8, -1]], np.float32))
    rows = np.concatenate([own, low, high], axis=1)
    per = 128 // slots
    source = np.arange(per * width).reshape(per, 2, slots, 2).transpose(3, 1, 0, 2).reshape(-1)
    permutation = np.zeros((per * width, per * width), np.float32)
    permutation[source, np.arange(per * width)] = 1.0
    return rows.astype(jnp.bfloat16), permutation.astype(jnp.bfloat16)


def dot(a, b, dims):
    return lax.dot_general(a, b, (dims, ((), ())), preferred_element_type=F32)


HERE = pl.BlockSpec(memory_space=pltpu.VMEM)
FAR = pl.BlockSpec(memory_space=pltpu.HBM)
SCALARS = pl.BlockSpec(memory_space=pltpu.SMEM)


def in_hbm(x):
    return pltpu.with_memory_space_constraint(x, pltpu.HBM)


def call(kernel, name, out_shape, in_specs, out_specs, scratch=(), limit=16):
    return pl.pallas_call(
        kernel,
        out_shape=out_shape,
        in_specs=in_specs,
        out_specs=out_specs,
        scratch_shapes=list(scratch),
        compiler_params=pltpu.CompilerParams(vmem_limit_bytes=limit << 20),
        name=name,
    )


def stage_kernel(x_ref, out_ref, held, sem):
    fields, parts, slots = held.shape[:3]
    copies = []
    for field in range(fields):
        for part in range(parts):
            for half in range(2):
                area = (field, part, pl.ds(half * (slots // 2), slots // 2))
                copies.append(pltpu.make_async_copy(
                    x_ref.at[area], held.at[area], sem.at[len(copies)]))
                copies[-1].start()
    rows = out_ref.shape[0] // fields
    for field in range(fields):
        for copy in copies[4 * field:4 * field + 4]:
            copy.wait()
        out_ref[field * rows:(field + 1) * rows, :] = held[field].reshape(rows, held.shape[-1])


def stage(x):
    rows, modes = 3 * math.prod(x.shape[1:-1]), x.shape[-1]
    return call(
        stage_kernel, "stage", pltpu.VMEM((rows, modes), BF16),
        [FAR], HERE, [pltpu.VMEM((3,) + x.shape[1:], BF16), pltpu.SemaphoreType.DMA((12,))],
    )(in_hbm(x))


def masked_rows(block, lens, weight):
    modes = lax.broadcasted_iota(jnp.int32, block.shape, 1)
    return jnp.where(modes < lens[:, :1], block.astype(F32) * weight[:, :1], 0.0).astype(BF16)


def send_bands(table_ref, rows, out_ref, buffer, sem, loads=None, count=4):
    size = table_ref.shape[0] // count
    copies = []
    for i in range(count):
        part = pl.ds(i * size, size)
        if loads is not None:
            loads[i].wait()
        buffer[part, :] = dot(table_ref[part, :], rows, ((1,), (1,))).astype(BF16)
        copies.append(pltpu.make_async_copy(buffer.at[part], out_ref.at[part], sem.at[i]))
        copies[-1].start()
    for copy in copies:
        copy.wait()


def slot_rows(orders, lengths, slots):
    index = lax.axis_index("order")
    per_row = 128 // slots
    lane = lax.broadcasted_iota(jnp.int32, (128, 128), 1)
    held = jnp.broadcast_to(orders[pl.ds(index // per_row, 1), :], (128, 128)).T
    total = jnp.zeros((128, 128), F32)
    for row in range(lengths.shape[0]):
        wide = jnp.broadcast_to(lengths[row:row + 1, :], (128, 128)).astype(F32)
        total += jnp.where(held == lane + row * 128, wide, 0.0)
    found = jnp.sum(total, axis=1, keepdims=True).astype(jnp.int32)
    found = jnp.broadcast_to(found, (128, 128))
    zero = jnp.where(held == 0, 1, 0)
    columns = jnp.where(lane == 0, found >> 3, jnp.where(lane == 1, found & 7, zero))
    rows = lax.broadcasted_iota(jnp.int32, (2 * slots, 128), 0) // 2
    picked = lax.broadcasted_iota(jnp.int32, (2 * slots, 128), 1)
    pick = jnp.where(picked == rows + (index % per_row) * slots, 1.0, 0.0).astype(BF16)
    result = dot(pick, columns.astype(F32).astype(BF16), ((1,), (0,)))
    lens = (result[:, 0:1] * 8.0 + result[:, 1:2]).astype(jnp.int32)
    weight = 2.0 - result[:, 2:3]
    return jnp.concatenate([lens, lens], axis=0), jnp.concatenate([weight, weight], axis=0)


def raw_kernel(orders_far, lengths_far, x_far, table_far, out_ref, lens_ref, weight_ref,
               buffer, sem, orders, lengths, x_ref, small_sem, table, load_sem):
    size = table.shape[0] // 4
    small = [
        pltpu.make_async_copy(orders_far, orders, small_sem.at[0]),
        pltpu.make_async_copy(lengths_far, lengths, small_sem.at[1]),
        pltpu.make_async_copy(x_far.at[3, 0], x_ref.at[0], small_sem.at[2]),
        pltpu.make_async_copy(x_far.at[3, 1], x_ref.at[1], small_sem.at[3]),
    ]
    loads = [
        pltpu.make_async_copy(table_far.at[pl.ds(i * size, size)],
                              table.at[pl.ds(i * size, size)], load_sem.at[i])
        for i in range(4)
    ]
    for copy in small + loads:
        copy.start()
    small[0].wait()
    small[1].wait()
    lens, weight = slot_rows(orders, lengths, x_ref.shape[1])
    lens_ref[...] = jnp.broadcast_to(lens, lens_ref.shape)
    weight_ref[...] = jnp.broadcast_to(weight, weight_ref.shape)
    small[2].wait()
    small[3].wait()
    block = x_ref[...]
    block = block.reshape(math.prod(block.shape[:-1]), block.shape[-1])
    send_bands(table, masked_rows(block, lens, weight), out_ref, buffer, sem, loads)


def radial_raw(orders, lengths, x, table):
    rows = math.prod(x.shape[1:-1])
    return call(
        raw_kernel, "radial_raw",
        (pltpu.HBM((R, rows), BF16),
         jax.ShapeDtypeStruct((rows, 128), jnp.int32),
         jax.ShapeDtypeStruct((rows, 128), F32)),
        [FAR] * 4, (FAR, HERE, HERE),
        [pltpu.VMEM((R, rows), BF16), pltpu.SemaphoreType.DMA((4,)),
         pltpu.VMEM(orders.shape, jnp.int32), pltpu.VMEM(lengths.shape, jnp.int32),
         pltpu.VMEM(x.shape[1:], BF16), pltpu.SemaphoreType.DMA((4,)),
         pltpu.VMEM(table.shape, BF16), pltpu.SemaphoreType.DMA((4,))],
    )(in_hbm(orders), in_hbm(lengths), in_hbm(x), in_hbm(table))


def row_loads(far_ref, held, sem, count=4):
    size = held.shape[0] // count
    loads = []
    for i in range(count):
        rows = pl.ds(i * size, size)
        loads.append(pltpu.make_async_copy(far_ref.at[rows], held.at[rows], sem.at[i]))
        loads[-1].start()
    return loads


def slope_kernel(x_ref, low_ref, high_ref, lens_ref, weight_ref, rows_ref, table_far, out_ref,
                 buffer, sem, table, load_sem):
    loads = row_loads(table_far, table, load_sem)
    held = []
    count = x_ref.shape[0] // 3
    for field in range(3):
        rows = pl.ds(field * count, count)
        stacked = jnp.concatenate([x_ref[rows, :], low_ref[rows, :], high_ref[rows, :]], axis=0)
        slope = dot(rows_ref[...], stacked, ((1,), (0,)))
        held.append(masked_rows(slope, lens_ref[...], weight_ref[...]))
    send_bands(table, jnp.concatenate(held, axis=0), out_ref, buffer, sem, loads)


def radial_slope(x, low, high, lens, weight, rows_map, table):
    rows = x.shape[0]
    return call(
        slope_kernel, "radial_slope", pltpu.HBM((R, rows), BF16), [HERE] * 6 + [FAR], FAR,
        [pltpu.VMEM((R, rows), BF16), pltpu.SemaphoreType.DMA((4,)),
         pltpu.VMEM(table.shape, BF16), pltpu.SemaphoreType.DMA((4,))],
    )(x, low, high, lens, weight, rows_map, in_hbm(table))


def sine_cosine(phase, points):
    centred = ((phase + points // 2) & (points - 1)) - points // 2
    y = centred.astype(F32) * (math.pi / points)
    square = y * y
    sine = jnp.float32(0.0)
    for n in (11, 9, 7, 5, 3, 1):
        sine = sine * square + (-1.0) ** (n // 2) / math.factorial(n)
    sine = sine * y
    cosine = jnp.float32(0.0)
    for n in (12, 10, 8, 6, 4, 2, 0):
        cosine = cosine * square + (-1.0) ** (n // 2) / math.factorial(n)
    return 1.0 - 2.0 * sine * sine, 2.0 * sine * cosine


def table_kernel(slots, orders_ref, far_ref, out_ref, sem):
    half = 128 * orders_ref.shape[0]
    points = 2 * half
    lane = lax.broadcasted_iota(jnp.int32, (slots, 128), 1)
    copies = []
    for row in range(orders_ref.shape[0]):
        column = jnp.broadcast_to(orders_ref[row:row + 1, :], (128, 128)).T
        for piece in range(128 // slots):
            orders = column[piece * slots:(piece + 1) * slots]
            rows = pl.ds(row * 128 + piece * slots, slots)
            cos_now, sin_now = sine_cosine((orders * lane) & (points - 1), points)
            cos_turn, sin_turn = sine_cosine((orders * 128) & (points - 1), points)
            for block in range(half // 128):
                out_ref[rows, pl.ds(block * 128, 128)] = cos_now.astype(BF16)
                out_ref[rows, pl.ds(half + (block + 1) * 128, 128)] = (-sin_now).astype(BF16)
                cos_now, sin_now = (
                    cos_now * cos_turn - sin_now * sin_turn,
                    sin_now * cos_turn + cos_now * sin_turn,
                )
            sign = jnp.where(lane == 0, 1 - 2 * (orders & 1), 0)
            out_ref[rows, pl.ds(half, 128)] = sign.astype(F32).astype(BF16)
        part = pl.ds(row * 128, 128)
        copies.append(pltpu.make_async_copy(out_ref.at[part], far_ref.at[part], sem.at[row]))
        copies[-1].start()
    for copy in copies:
        copy.wait()


def azimuthal_table(orders, slots):
    shape = (orders.size, 2 * orders.size + 128)
    return call(
        functools.partial(table_kernel, slots), "azimuthal_table",
        pltpu.HBM(shape, BF16), [HERE], FAR,
        [pltpu.VMEM(shape, BF16), pltpu.SemaphoreType.DMA((orders.shape[0],))],
    )(orders)


def place_field(lhs, row, bands, perm_ref, groups, band):
    per = perm_ref.shape[0] // bands.shape[1]
    stacked = jnp.concatenate([
        jnp.concatenate(
            [bands[(tile * per + e) * band:(tile * per + e + 1) * band] for e in range(per)], axis=1
        )
        for tile in range(groups // per)
    ], axis=0)
    mapped = dot(stacked, perm_ref[...], ((1,), (0,))).astype(BF16)
    for tile in range(groups // per):
        for plane in range(2):
            for part in range(2):
                lanes = (2 * plane + part) * 128
                lhs[part, row + plane * band:row + (plane + 1) * band,
                    pl.ds(tile * 128, 128)] = mapped[tile * band:(tile + 1) * band,
                                                     lanes:lanes + 128]


def table_loads(far_ref, table_ref, sem):
    rows, columns = table_ref.shape
    half = rows
    step = half // 2
    pieces = [(0, step), (half + 128, step), (step, step + 128), (half + 128 + step, step)]
    loads = []
    for start, size in pieces:
        loads.append([])
        for piece in range(4):
            area = (pl.ds(piece * (rows // 4), rows // 4), pl.ds(start, size))
            index = 4 * (len(loads) - 1) + piece
            loads[-1].append(pltpu.make_async_copy(
                far_ref.at[area], table_ref.at[area], sem.at[index]))
            loads[-1][-1].start()
    return pieces, loads


def axial_kernel(groups, band, raw_ref, perm_ref, far_ref, axial_ref, lhs, table_ref, sem):
    pieces, loads = table_loads(far_ref, table_ref, sem)
    place_field(lhs, 0, raw_ref[...], perm_ref, groups, band)
    half = table_ref.shape[0]
    for index, (start, size) in enumerate(pieces):
        for load in loads[index]:
            load.wait()
        part = pl.ds(start, size)
        values = dot(lhs[index % 2], table_ref[:, part], ((1,), (0,)))
        column = lax.broadcasted_iota(jnp.int32, values.shape, 1) + start
        once = (column == 0) | (column == half)
        axial_ref[:, part] = values * jnp.where(once, 1.0 / 12.0, 1.0 / 6.0)


def axial_stage(raw, perm, table, groups, band):
    rows, columns = table.shape
    return call(
        functools.partial(axial_kernel, groups, band), "axial_stage",
        jax.ShapeDtypeStruct((2 * band, columns), F32),
        [HERE, HERE, FAR], HERE,
        [pltpu.VMEM((2, 2 * band, rows), BF16), pltpu.VMEM(table.shape, BF16),
         pltpu.SemaphoreType.DMA((16,))],
    )(raw, perm, in_hbm(table))


def physical_kernel(groups, band, step, scale, slope_ref, axial_ref, perm_ref, far_ref, out_ref,
                    lhs, even, odd, table_ref, sem):
    pieces, loads = table_loads(far_ref, table_ref, sem)
    width = slope_ref.shape[1] // 3
    half = table_ref.shape[0]
    per = perm_ref.shape[0] // width
    for field in range(3):
        place_field(lhs, 2 * field * band, slope_ref[:, field * width:(field + 1) * width],
                    perm_ref, groups, band)
    for index in (0, 2):
        (start, size), (other, span) = pieces[index], pieces[index + 1]
        for load in loads[index]:
            load.wait()
        cosines = dot(lhs[0], table_ref[:, pl.ds(start, size)], ((1,), (0,)))
        for load in loads[index + 1]:
            load.wait()
        sines = dot(lhs[1], table_ref[:, pl.ds(other, span)], ((1,), (0,)))
        axial_cos = axial_ref[:, pl.ds(start, size)]
        axial_sin = axial_ref[:, pl.ds(other, span)]
        for g in range(3):
            area = slice(2 * g * band, (2 * g + 2) * band)
            c, s = cosines[area], sines[area]
            part = pl.ds(start, span)
            even[area, part] = (c[:, :span] * axial_cos[:, :span] + s * axial_sin).astype(BF16)
            odd[area, part] = (c[:, :span] * axial_sin + s * axial_cos[:, :span]).astype(BF16)
            if size > span:
                edge = (c[:, span:] * axial_cos[:, span:]).astype(BF16)
                even[area, pl.ds(start + span, size - span)] = edge

    for start in range(0, half, step):
        rows = pl.ds(start, step)
        parts = [
            (dot(even[...], table_ref[rows, 0:half + 128], ((1,), (1,))) * scale).astype(BF16),
            (dot(odd[...], table_ref[rows, half + 128:], ((1,), (1,))) * scale).astype(BF16),
        ]
        stacked = jnp.concatenate([
            jnp.concatenate([
                parts[part][(2 * g + plane) * band:(2 * g + plane + 1) * band,
                            tile * 128:(tile + 1) * 128]
                for plane in range(2) for part in range(2)
            ], axis=1)
            for g in range(3) for tile in range(step // 128)
        ], axis=0)
        mapped = dot(stacked, perm_ref[...], ((1,), (1,))).astype(BF16)
        for g in range(3):
            for tile in range(step // 128):
                source = (g * (step // 128) + tile) * band
                for e in range(per):
                    row = ((start // 128 + tile) * per + e) * band
                    out_ref[row:row + band, pl.ds(g * width, width)] = mapped[
                        source:source + band, e * width:(e + 1) * width]


def physical_stage(slope, axial, perm, table, groups, band, step=512):
    rows = table.shape[0]
    scale = math.sqrt(1.0 / rows)
    return call(
        functools.partial(physical_kernel, groups, band, step, scale), "physical_stage",
        jax.ShapeDtypeStruct(slope.shape, BF16), [HERE] * 3 + [FAR], HERE,
        [pltpu.VMEM((2, 6 * band, rows), BF16), pltpu.VMEM((6 * band, rows + 128), BF16),
         pltpu.VMEM((6 * band, rows), BF16), pltpu.VMEM(table.shape, BF16),
         pltpu.SemaphoreType.DMA((16,))],
        limit=28,
    )(slope, axial, perm, in_hbm(table))


def final_kernel(x_ref, lens_ref, table_ref, out_ref, buffer, sem):
    width = x_ref.shape[1] // 3
    modes = lax.broadcasted_iota(jnp.int32, (width, table_ref.shape[1]), 1)
    keep = modes < lens_ref[:, :1]
    copies = []
    for g in range(3):
        part = x_ref[:, g * width:(g + 1) * width]
        result = dot(part, table_ref[...], ((0,), (0,)))
        rows = jnp.where(keep, result, 0.0).astype(BF16)
        buffer[g] = rows.reshape(buffer.shape[1:])
        copies.append(pltpu.make_async_copy(buffer.at[g], out_ref.at[g], sem.at[g]))
        copies[-1].start()
    for copy in copies:
        copy.wait()


def radial_analysis(x, lens, table, shape):
    return call(
        final_kernel, "radial_analysis", pltpu.HBM(shape, BF16), [HERE] * 3, FAR,
        [pltpu.VMEM(shape, BF16), pltpu.SemaphoreType.DMA((3,))],
    )(x, lens, table)


def shift(block, offset):
    count = lax.axis_size("axial")
    return lax.ppermute(block, "axial", [(i, (i + offset) % count) for i in range(count)])


def exchange(block):
    return lax.all_to_all(block, "order", split_axis=0, concat_axis=0, tiled=True)


def shards(coefficients, order_lists, lengths):
    field_count, part_count, slots, planes, modes = coefficients.shape
    order_count = order_lists.shape[0]
    groups = lax.axis_size("order")
    band = R // groups
    width = part_count * slots * planes
    synthesis, analysis = radial_constants(R, modes)
    rows_map, perm = plane_matrices(slots)

    sloped = stage(coefficients)
    low, high = shift(sloped, 1), shift(sloped, -1)
    orders = order_lists.reshape(order_count // 128, 128)
    bands, lens, weight = radial_raw(
        orders, lengths.reshape(order_count // 128, 128), coefficients, synthesis
    )
    raw_bands = exchange(bands)
    table = azimuthal_table(orders, slots)
    slope_bands = exchange(
        radial_slope(sloped, low, high, lens, weight, rows_map, synthesis)
    )
    axial = axial_stage(raw_bands, perm, table, groups, band)
    spectral = physical_stage(slope_bands, axial, perm, table, groups, band)
    shape = (3, part_count, slots, planes, modes)
    return radial_analysis(exchange(spectral), lens, analysis, shape)


def solution(mesh):
    placed = (P(None, None, "order", "axial", None), P(), P())
    return jax.shard_map(
        shards,
        mesh=mesh,
        in_specs=placed,
        out_specs=P(None, None, "order", "axial", None),
        check_vma=False,
    )
```

```python
import functools
import math

import jax
import jax.numpy as jnp
import numpy as np
from jax import lax
from jax.experimental import pallas as pl
from jax.experimental.pallas import tpu as pltpu
from jax.sharding import PartitionSpec as P

R = 1024
F32 = jnp.float32
BF16 = jnp.bfloat16


def radial_constants(radius_count, mode_count):
    radius_ids = np.arange(radius_count)
    mode_ids = np.arange(mode_count)
    phases = mode_ids[None, :] * (2 * radius_ids[:, None] + 1) % (4 * radius_count)
    cosines = np.cos(phases * (math.pi / (2 * radius_count))).astype(np.float32)
    synthesis = cosines.astype(jnp.bfloat16)
    analysis = (cosines * np.float32(math.sqrt(2.0 / radius_count))).astype(jnp.bfloat16)
    return synthesis, analysis


def plane_matrices(slots):
    width = 2 * slots * 2
    eye = np.eye(width // 2, dtype=np.float32)
    own = np.kron(eye, np.array([[0, 8], [-8, 0]], np.float32))
    low = np.kron(eye, np.array([[1, -8], [0, 1]], np.float32))
    high = np.kron(eye, np.array([[-1, 0], [8, -1]], np.float32))
    rows = np.concatenate([own, low, high], axis=1)
    per = 128 // slots
    source = np.arange(per * width).reshape(per, 2, slots, 2).transpose(3, 1, 0, 2).reshape(-1)
    permutation = np.zeros((per * width, per * width), np.float32)
    permutation[source, np.arange(per * width)] = 1.0
    return rows.astype(jnp.bfloat16), permutation.astype(jnp.bfloat16)


def dot(a, b, dims):
    return lax.dot_general(a, b, (dims, ((), ())), preferred_element_type=F32)


HERE = pl.BlockSpec(memory_space=pltpu.VMEM)
FAR = pl.BlockSpec(memory_space=pltpu.HBM)
SCALARS = pl.BlockSpec(memory_space=pltpu.SMEM)


def in_hbm(x):
    return pltpu.with_memory_space_constraint(x, pltpu.HBM)


def call(kernel, name, out_shape, in_specs, out_specs, scratch=(), limit=16):
    return pl.pallas_call(
        kernel,
        out_shape=out_shape,
        in_specs=in_specs,
        out_specs=out_specs,
        scratch_shapes=list(scratch),
        compiler_params=pltpu.CompilerParams(vmem_limit_bytes=limit << 20),
        name=name,
    )


def stage_kernel(x_ref, out_ref, held, sem):
    fields, parts, slots = held.shape[:3]
    copies = []
    for field in range(fields):
        for part in range(parts):
            for half in range(2):
                area = (field, part, pl.ds(half * (slots // 2), slots // 2))
                copies.append(pltpu.make_async_copy(
                    x_ref.at[area], held.at[area], sem.at[len(copies)]))
                copies[-1].start()
    rows = out_ref.shape[0] // fields
    for field in range(fields):
        for copy in copies[4 * field:4 * field + 4]:
            copy.wait()
        out_ref[field * rows:(field + 1) * rows, :] = held[field].reshape(rows, held.shape[-1])


def stage(x):
    rows, modes = 3 * math.prod(x.shape[1:-1]), x.shape[-1]
    return call(
        stage_kernel, "stage", pltpu.VMEM((rows, modes), BF16),
        [FAR], HERE, [pltpu.VMEM((3,) + x.shape[1:], BF16), pltpu.SemaphoreType.DMA((12,))],
    )(in_hbm(x))


def masked_rows(block, lens, weight):
    modes = lax.broadcasted_iota(jnp.int32, block.shape, 1)
    return jnp.where(modes < lens[:, :1], block.astype(F32) * weight[:, :1], 0.0).astype(BF16)


def row_loads(far_ref, held, sem, count=16):
    size = held.shape[0] // count
    loads = []
    for i in range(count):
        rows = pl.ds(i * size, size)
        loads.append(pltpu.make_async_copy(far_ref.at[rows], held.at[rows], sem.at[i]))
        loads[-1].start()
    return loads


def send_bands(table_ref, rows, out_ref, buffer, sem, loads=None, count=4):
    size = table_ref.shape[0] // count
    copies = []
    for i in range(count):
        part = pl.ds(i * size, size)
        if loads is not None:
            share = len(loads) // count
            for load in loads[i * share:(i + 1) * share]:
                load.wait()
        buffer[part, :] = dot(table_ref[part, :], rows, ((1,), (1,))).astype(BF16)
        copies.append(pltpu.make_async_copy(buffer.at[part], out_ref.at[part], sem.at[i]))
        copies[-1].start()
    for copy in copies:
        copy.wait()


def slot_rows(orders, lengths, slots):
    index = lax.axis_index("order")
    per_row = 128 // slots
    lane = lax.broadcasted_iota(jnp.int32, (128, 128), 1)
    held = jnp.broadcast_to(orders[pl.ds(index // per_row, 1), :], (128, 128)).T
    total = jnp.zeros((128, 128), F32)
    for row in range(lengths.shape[0]):
        wide = jnp.broadcast_to(lengths[row:row + 1, :], (128, 128)).astype(F32)
        total += jnp.where(held == lane + row * 128, wide, 0.0)
    found = jnp.sum(total, axis=1, keepdims=True).astype(jnp.int32)
    found = jnp.broadcast_to(found, (128, 128))
    zero = jnp.where(held == 0, 1, 0)
    columns = jnp.where(lane == 0, found >> 3, jnp.where(lane == 1, found & 7, zero))
    rows = lax.broadcasted_iota(jnp.int32, (2 * slots, 128), 0) // 2
    picked = lax.broadcasted_iota(jnp.int32, (2 * slots, 128), 1)
    pick = jnp.where(picked == rows + (index % per_row) * slots, 1.0, 0.0).astype(BF16)
    result = dot(pick, columns.astype(F32).astype(BF16), ((1,), (0,)))
    lens = (result[:, 0:1] * 8.0 + result[:, 1:2]).astype(jnp.int32)
    weight = 2.0 - result[:, 2:3]
    return jnp.concatenate([lens, lens], axis=0), jnp.concatenate([weight, weight], axis=0)


def raw_kernel(orders_far, lengths_far, x_far, table_far, out_ref, lens_ref, weight_ref,
               buffer, sem, orders, lengths, x_ref, small_sem, table, load_sem):
    small = [
        pltpu.make_async_copy(orders_far, orders, small_sem.at[0]),
        pltpu.make_async_copy(lengths_far, lengths, small_sem.at[1]),
        pltpu.make_async_copy(x_far.at[3, 0], x_ref.at[0], small_sem.at[2]),
        pltpu.make_async_copy(x_far.at[3, 1], x_ref.at[1], small_sem.at[3]),
    ]
    for copy in small:
        copy.start()
    loads = row_loads(table_far, table, load_sem)
    small[0].wait()
    small[1].wait()
    lens, weight = slot_rows(orders, lengths, x_ref.shape[1])
    lens_ref[...] = jnp.broadcast_to(lens, lens_ref.shape)
    weight_ref[...] = jnp.broadcast_to(weight, weight_ref.shape)
    small[2].wait()
    small[3].wait()
    block = x_ref[...]
    block = block.reshape(math.prod(block.shape[:-1]), block.shape[-1])
    send_bands(table, masked_rows(block, lens, weight), out_ref, buffer, sem, loads)


def radial_raw(orders, lengths, x, table):
    rows = math.prod(x.shape[1:-1])
    return call(
        raw_kernel, "radial_raw",
        (pltpu.HBM((R, rows), BF16),
         jax.ShapeDtypeStruct((rows, 128), jnp.int32),
         jax.ShapeDtypeStruct((rows, 128), F32)),
        [FAR] * 4, (FAR, HERE, HERE),
        [pltpu.VMEM((R, rows), BF16), pltpu.SemaphoreType.DMA((4,)),
         pltpu.VMEM(orders.shape, jnp.int32), pltpu.VMEM(lengths.shape, jnp.int32),
         pltpu.VMEM(x.shape[1:], BF16), pltpu.SemaphoreType.DMA((4,)),
         pltpu.VMEM(table.shape, BF16), pltpu.SemaphoreType.DMA((16,))],
    )(in_hbm(orders), in_hbm(lengths), in_hbm(x), in_hbm(table))


def slope_kernel(x_ref, low_ref, high_ref, lens_ref, weight_ref, rows_ref, table_far, out_ref,
                 buffer, sem, table, load_sem):
    loads = row_loads(table_far, table, load_sem)
    held = []
    count = x_ref.shape[0] // 3
    for field in range(3):
        rows = pl.ds(field * count, count)
        stacked = jnp.concatenate([x_ref[rows, :], low_ref[rows, :], high_ref[rows, :]], axis=0)
        slope = dot(rows_ref[...], stacked, ((1,), (0,)))
        held.append(masked_rows(slope, lens_ref[...], weight_ref[...]))
    send_bands(table, jnp.concatenate(held, axis=0), out_ref, buffer, sem, loads)


def radial_slope(x, low, high, lens, weight, rows_map, table):
    rows = x.shape[0]
    return call(
        slope_kernel, "radial_slope", pltpu.HBM((R, rows), BF16), [HERE] * 6 + [FAR], FAR,
        [pltpu.VMEM((R, rows), BF16), pltpu.SemaphoreType.DMA((4,)),
         pltpu.VMEM(table.shape, BF16), pltpu.SemaphoreType.DMA((16,))],
    )(x, low, high, lens, weight, rows_map, in_hbm(table))


def sine_cosine(phase, points):
    centred = ((phase + points // 2) & (points - 1)) - points // 2
    y = centred.astype(F32) * (math.pi / points)
    square = y * y
    sine = jnp.float32(0.0)
    for n in (11, 9, 7, 5, 3, 1):
        sine = sine * square + (-1.0) ** (n // 2) / math.factorial(n)
    sine = sine * y
    cosine = jnp.float32(0.0)
    for n in (12, 10, 8, 6, 4, 2, 0):
        cosine = cosine * square + (-1.0) ** (n // 2) / math.factorial(n)
    return 1.0 - 2.0 * sine * sine, 2.0 * sine * cosine


def table_kernel(slots, orders_ref, far_ref, out_ref, sem):
    half = 128 * orders_ref.shape[0]
    points = 2 * half
    lane = lax.broadcasted_iota(jnp.int32, (slots, 128), 1)
    copies = []
    for row in range(orders_ref.shape[0]):
        column = jnp.broadcast_to(orders_ref[row:row + 1, :], (128, 128)).T
        for piece in range(128 // slots):
            orders = column[piece * slots:(piece + 1) * slots]
            rows = pl.ds(row * 128 + piece * slots, slots)
            cos_now, sin_now = sine_cosine((orders * lane) & (points - 1), points)
            cos_turn, sin_turn = sine_cosine((orders * 128) & (points - 1), points)
            for block in range(half // 128):
                out_ref[rows, pl.ds(block * 128, 128)] = cos_now.astype(BF16)
                out_ref[rows, pl.ds(half + (block + 1) * 128, 128)] = (-sin_now).astype(BF16)
                cos_now, sin_now = (
                    cos_now * cos_turn - sin_now * sin_turn,
                    sin_now * cos_turn + cos_now * sin_turn,
                )
            sign = jnp.where(lane == 0, 1 - 2 * (orders & 1), 0)
            out_ref[rows, pl.ds(half, 128)] = sign.astype(F32).astype(BF16)
        part = pl.ds(row * 128, 128)
        copies.append(pltpu.make_async_copy(out_ref.at[part], far_ref.at[part], sem.at[row]))
        copies[-1].start()
    for copy in copies:
        copy.wait()


def azimuthal_table(orders, slots):
    shape = (orders.size, 2 * orders.size + 128)
    return call(
        functools.partial(table_kernel, slots), "azimuthal_table",
        pltpu.HBM(shape, BF16), [HERE], FAR,
        [pltpu.VMEM(shape, BF16), pltpu.SemaphoreType.DMA((orders.shape[0],))],
    )(orders)


def place_field(lhs, row, bands, perm_ref, groups, band):
    per = perm_ref.shape[0] // bands.shape[1]
    stacked = jnp.concatenate([
        jnp.concatenate(
            [bands[(tile * per + e) * band:(tile * per + e + 1) * band] for e in range(per)], axis=1
        )
        for tile in range(groups // per)
    ], axis=0)
    mapped = dot(stacked, perm_ref[...], ((1,), (0,))).astype(BF16)
    for tile in range(groups // per):
        for plane in range(2):
            for part in range(2):
                lanes = (2 * plane + part) * 128
                lhs[part, row + plane * band:row + (plane + 1) * band,
                    pl.ds(tile * 128, 128)] = mapped[tile * band:(tile + 1) * band,
                                                     lanes:lanes + 128]


def table_loads(far_ref, table_ref, sem):
    rows, columns = table_ref.shape
    half = rows
    step = half // 2
    pieces = [(0, step), (half + 128, step), (step, step + 128), (half + 128 + step, step)]
    loads = []
    for start, size in pieces:
        loads.append([])
        for piece in range(4):
            area = (pl.ds(piece * (rows // 4), rows // 4), pl.ds(start, size))
            index = 4 * (len(loads) - 1) + piece
            loads[-1].append(pltpu.make_async_copy(
                far_ref.at[area], table_ref.at[area], sem.at[index]))
            loads[-1][-1].start()
    return pieces, loads


def axial_kernel(groups, band, raw_ref, perm_ref, far_ref, axial_ref, lhs, table_ref, sem):
    pieces, loads = table_loads(far_ref, table_ref, sem)
    place_field(lhs, 0, raw_ref[...], perm_ref, groups, band)
    half = table_ref.shape[0]
    for index, (start, size) in enumerate(pieces):
        for load in loads[index]:
            load.wait()
        part = pl.ds(start, size)
        values = dot(lhs[index % 2], table_ref[:, part], ((1,), (0,)))
        column = lax.broadcasted_iota(jnp.int32, values.shape, 1) + start
        once = (column == 0) | (column == half)
        axial_ref[:, part] = values * jnp.where(once, 1.0 / 12.0, 1.0 / 6.0)


def axial_stage(raw, perm, table, groups, band):
    rows, columns = table.shape
    return call(
        functools.partial(axial_kernel, groups, band), "axial_stage",
        jax.ShapeDtypeStruct((2 * band, columns), F32),
        [HERE, HERE, FAR], HERE,
        [pltpu.VMEM((2, 2 * band, rows), BF16), pltpu.VMEM(table.shape, BF16),
         pltpu.SemaphoreType.DMA((16,))],
    )(raw, perm, in_hbm(table))


def physical_kernel(groups, band, step, scale, slope_ref, axial_ref, perm_ref, far_ref, out_ref,
                    lhs, even, odd, table_ref, sem):
    pieces, loads = table_loads(far_ref, table_ref, sem)
    width = slope_ref.shape[1] // 3
    half = table_ref.shape[0]
    per = perm_ref.shape[0] // width
    for field in range(3):
        place_field(lhs, 2 * field * band, slope_ref[:, field * width:(field + 1) * width],
                    perm_ref, groups, band)
    for index in (0, 2):
        (start, size), (other, span) = pieces[index], pieces[index + 1]
        for load in loads[index]:
            load.wait()
        cosines = dot(lhs[0], table_ref[:, pl.ds(start, size)], ((1,), (0,)))
        for load in loads[index + 1]:
            load.wait()
        sines = dot(lhs[1], table_ref[:, pl.ds(other, span)], ((1,), (0,)))
        axial_cos = axial_ref[:, pl.ds(start, size)]
        axial_sin = axial_ref[:, pl.ds(other, span)]
        for g in range(3):
            area = slice(2 * g * band, (2 * g + 2) * band)
            c, s = cosines[area], sines[area]
            part = pl.ds(start, span)
            even[area, part] = (c[:, :span] * axial_cos[:, :span] + s * axial_sin).astype(BF16)
            odd[area, part] = (c[:, :span] * axial_sin + s * axial_cos[:, :span]).astype(BF16)
            if size > span:
                edge = (c[:, span:] * axial_cos[:, span:]).astype(BF16)
                even[area, pl.ds(start + span, size - span)] = edge

    for start in range(0, half, step):
        rows = pl.ds(start, step)
        parts = [
            (dot(even[...], table_ref[rows, 0:half + 128], ((1,), (1,))) * scale).astype(BF16),
            (dot(odd[...], table_ref[rows, half + 128:], ((1,), (1,))) * scale).astype(BF16),
        ]
        stacked = jnp.concatenate([
            jnp.concatenate([
                parts[part][(2 * g + plane) * band:(2 * g + plane + 1) * band,
                            tile * 128:(tile + 1) * 128]
                for plane in range(2) for part in range(2)
            ], axis=1)
            for g in range(3) for tile in range(step // 128)
        ], axis=0)
        mapped = dot(stacked, perm_ref[...], ((1,), (1,))).astype(BF16)
        for g in range(3):
            for tile in range(step // 128):
                source = (g * (step // 128) + tile) * band
                for e in range(per):
                    row = ((start // 128 + tile) * per + e) * band
                    out_ref[row:row + band, pl.ds(g * width, width)] = mapped[
                        source:source + band, e * width:(e + 1) * width]


def physical_stage(slope, axial, perm, table, groups, band, step=512):
    rows = table.shape[0]
    scale = math.sqrt(1.0 / rows)
    return call(
        functools.partial(physical_kernel, groups, band, step, scale), "physical_stage",
        jax.ShapeDtypeStruct(slope.shape, BF16), [HERE] * 3 + [FAR], HERE,
        [pltpu.VMEM((2, 6 * band, rows), BF16), pltpu.VMEM((6 * band, rows + 128), BF16),
         pltpu.VMEM((6 * band, rows), BF16), pltpu.VMEM(table.shape, BF16),
         pltpu.SemaphoreType.DMA((16,))],
        limit=28,
    )(slope, axial, perm, in_hbm(table))


def final_kernel(x_ref, lens_ref, table_ref, out_ref, buffer, sem):
    width = x_ref.shape[1] // 3
    modes = lax.broadcasted_iota(jnp.int32, (width, table_ref.shape[1]), 1)
    keep = modes < lens_ref[:, :1]
    copies = []
    for g in range(3):
        part = x_ref[:, g * width:(g + 1) * width]
        result = dot(part, table_ref[...], ((0,), (0,)))
        rows = jnp.where(keep, result, 0.0).astype(BF16)
        buffer[g] = rows.reshape(buffer.shape[1:])
        copies.append(pltpu.make_async_copy(buffer.at[g], out_ref.at[g], sem.at[g]))
        copies[-1].start()
    for copy in copies:
        copy.wait()


def radial_analysis(x, lens, table, shape):
    return call(
        final_kernel, "radial_analysis", pltpu.HBM(shape, BF16), [HERE] * 3, FAR,
        [pltpu.VMEM(shape, BF16), pltpu.SemaphoreType.DMA((3,))],
    )(x, lens, table)


def shift(block, offset):
    count = lax.axis_size("axial")
    return lax.ppermute(block, "axial", [(i, (i + offset) % count) for i in range(count)])


def exchange(block):
    return lax.all_to_all(block, "order", split_axis=0, concat_axis=0, tiled=True)


def shards(coefficients, order_lists, lengths):
    field_count, part_count, slots, planes, modes = coefficients.shape
    order_count = order_lists.shape[0]
    groups = lax.axis_size("order")
    band = R // groups
    width = part_count * slots * planes
    synthesis, analysis = radial_constants(R, modes)
    rows_map, perm = plane_matrices(slots)

    sloped = stage(coefficients)
    low, high = shift(sloped, 1), shift(sloped, -1)
    orders = order_lists.reshape(order_count // 128, 128)
    bands, lens, weight = radial_raw(
        orders, lengths.reshape(order_count // 128, 128), coefficients, synthesis
    )
    raw_bands = exchange(bands)
    table = azimuthal_table(orders, slots)
    slope_bands = exchange(
        radial_slope(sloped, low, high, lens, weight, rows_map, synthesis)
    )
    axial = axial_stage(raw_bands, perm, table, groups, band)
    spectral = physical_stage(slope_bands, axial, perm, table, groups, band)
    shape = (3, part_count, slots, planes, modes)
    return radial_analysis(exchange(spectral), lens, analysis, shape)


def solution(mesh):
    placed = (P(None, None, "order", "axial", None), P(), P())
    return jax.shard_map(
        shards,
        mesh=mesh,
        in_specs=placed,
        out_specs=P(None, None, "order", "axial", None),
        check_vma=False,
    )
```

```python
import functools
import math

import jax
import jax.numpy as jnp
import numpy as np
from jax import lax
from jax.experimental import pallas as pl
from jax.experimental.pallas import tpu as pltpu
from jax.sharding import PartitionSpec as P

R = 1024
F32 = jnp.float32
BF16 = jnp.bfloat16


def radial_constants(radius_count, mode_count):
    radius_ids = np.arange(radius_count)
    mode_ids = np.arange(mode_count)
    phases = mode_ids[None, :] * (2 * radius_ids[:, None] + 1) % (4 * radius_count)
    cosines = np.cos(phases * (math.pi / (2 * radius_count))).astype(np.float32)
    synthesis = cosines.astype(jnp.bfloat16)
    analysis = (cosines * np.float32(math.sqrt(2.0 / radius_count))).astype(jnp.bfloat16)
    return synthesis, analysis


def plane_matrices(slots):
    width = 2 * slots * 2
    eye = np.eye(width // 2, dtype=np.float32)
    own = np.kron(eye, np.array([[0, 8], [-8, 0]], np.float32))
    low = np.kron(eye, np.array([[1, -8], [0, 1]], np.float32))
    high = np.kron(eye, np.array([[-1, 0], [8, -1]], np.float32))
    rows = np.concatenate([own, low, high], axis=1)
    per = 128 // slots
    source = np.arange(per * width).reshape(per, 2, slots, 2).transpose(3, 1, 0, 2).reshape(-1)
    permutation = np.zeros((per * width, per * width), np.float32)
    permutation[source, np.arange(per * width)] = 1.0
    return rows.astype(jnp.bfloat16), permutation.astype(jnp.bfloat16)


def dot(a, b, dims):
    return lax.dot_general(a, b, (dims, ((), ())), preferred_element_type=F32)


HERE = pl.BlockSpec(memory_space=pltpu.VMEM)
FAR = pl.BlockSpec(memory_space=pltpu.HBM)
SCALARS = pl.BlockSpec(memory_space=pltpu.SMEM)


def in_hbm(x):
    return pltpu.with_memory_space_constraint(x, pltpu.HBM)


def call(kernel, name, out_shape, in_specs, out_specs, scratch=(), limit=16):
    return pl.pallas_call(
        kernel,
        out_shape=out_shape,
        in_specs=in_specs,
        out_specs=out_specs,
        scratch_shapes=list(scratch),
        compiler_params=pltpu.CompilerParams(vmem_limit_bytes=limit << 20),
        name=name,
    )


def stage_kernel(x_ref, out_ref, held, sem):
    fields, parts, slots = held.shape[:3]
    copies = []
    for field in range(fields):
        for part in range(parts):
            for half in range(2):
                area = (field, part, pl.ds(half * (slots // 2), slots // 2))
                copies.append(pltpu.make_async_copy(
                    x_ref.at[area], held.at[area], sem.at[len(copies)]))
                copies[-1].start()
    rows = out_ref.shape[0] // fields
    for field in range(fields):
        for copy in copies[4 * field:4 * field + 4]:
            copy.wait()
        out_ref[field * rows:(field + 1) * rows, :] = held[field].reshape(rows, held.shape[-1])


def stage(x):
    rows, modes = 3 * math.prod(x.shape[1:-1]), x.shape[-1]
    return call(
        stage_kernel, "stage", pltpu.VMEM((rows, modes), BF16),
        [FAR], HERE, [pltpu.VMEM((3,) + x.shape[1:], BF16), pltpu.SemaphoreType.DMA((12,))],
    )(in_hbm(x))


def masked_rows(block, lens, weight):
    modes = lax.broadcasted_iota(jnp.int32, block.shape, 1)
    return jnp.where(modes < lens[:, :1], block.astype(F32) * weight[:, :1], 0.0).astype(BF16)


def send_bands(table_ref, rows, out_ref, buffer, sem, loads=None, count=4):
    size = table_ref.shape[0] // count
    copies = []
    for i in range(count):
        part = pl.ds(i * size, size)
        if loads is not None:
            loads[i].wait()
        buffer[part, :] = dot(table_ref[part, :], rows, ((1,), (1,))).astype(BF16)
        copies.append(pltpu.make_async_copy(buffer.at[part], out_ref.at[part], sem.at[i]))
        copies[-1].start()
    for copy in copies:
        copy.wait()


def slot_rows(orders, lengths, slots):
    index = lax.axis_index("order")
    per_row = 128 // slots
    lane = lax.broadcasted_iota(jnp.int32, (128, 128), 1)
    held = jnp.broadcast_to(orders[pl.ds(index // per_row, 1), :], (128, 128)).T
    total = jnp.zeros((128, 128), F32)
    for row in range(lengths.shape[0]):
        wide = jnp.broadcast_to(lengths[row:row + 1, :], (128, 128)).astype(F32)
        total += jnp.where(held == lane + row * 128, wide, 0.0)
    found = jnp.sum(total, axis=1, keepdims=True).astype(jnp.int32)
    found = jnp.broadcast_to(found, (128, 128))
    zero = jnp.where(held == 0, 1, 0)
    columns = jnp.where(lane == 0, found >> 3, jnp.where(lane == 1, found & 7, zero))
    rows = lax.broadcasted_iota(jnp.int32, (2 * slots, 128), 0) // 2
    picked = lax.broadcasted_iota(jnp.int32, (2 * slots, 128), 1)
    pick = jnp.where(picked == rows + (index % per_row) * slots, 1.0, 0.0).astype(BF16)
    result = dot(pick, columns.astype(F32).astype(BF16), ((1,), (0,)))
    lens = (result[:, 0:1] * 8.0 + result[:, 1:2]).astype(jnp.int32)
    weight = 2.0 - result[:, 2:3]
    return jnp.concatenate([lens, lens], axis=0), jnp.concatenate([weight, weight], axis=0)


def raw_kernel(orders_far, lengths_far, x_far, table_far, out_ref, lens_ref, weight_ref,
               buffer, sem, orders, lengths, x_ref, small_sem, table, load_sem):
    size = table.shape[0] // 4
    small = [
        pltpu.make_async_copy(orders_far, orders, small_sem.at[0]),
        pltpu.make_async_copy(lengths_far, lengths, small_sem.at[1]),
        pltpu.make_async_copy(x_far.at[3, 0], x_ref.at[0], small_sem.at[2]),
        pltpu.make_async_copy(x_far.at[3, 1], x_ref.at[1], small_sem.at[3]),
    ]
    loads = [
        pltpu.make_async_copy(table_far.at[pl.ds(i * size, size)],
                              table.at[pl.ds(i * size, size)], load_sem.at[i])
        for i in range(4)
    ]
    for copy in small + loads:
        copy.start()
    small[0].wait()
    small[1].wait()
    lens, weight = slot_rows(orders, lengths, x_ref.shape[1])
    lens_ref[...] = jnp.broadcast_to(lens, lens_ref.shape)
    weight_ref[...] = jnp.broadcast_to(weight, weight_ref.shape)
    small[2].wait()
    small[3].wait()
    block = x_ref[...]
    block = block.reshape(math.prod(block.shape[:-1]), block.shape[-1])
    send_bands(table, masked_rows(block, lens, weight), out_ref, buffer, sem, loads)


def radial_raw(orders, lengths, x, table):
    rows = math.prod(x.shape[1:-1])
    return call(
        raw_kernel, "radial_raw",
        (pltpu.HBM((R, rows), BF16),
         jax.ShapeDtypeStruct((rows, 128), jnp.int32),
         jax.ShapeDtypeStruct((rows, 128), F32)),
        [FAR] * 4, (FAR, HERE, HERE),
        [pltpu.VMEM((R, rows), BF16), pltpu.SemaphoreType.DMA((4,)),
         pltpu.VMEM(orders.shape, jnp.int32), pltpu.VMEM(lengths.shape, jnp.int32),
         pltpu.VMEM(x.shape[1:], BF16), pltpu.SemaphoreType.DMA((4,)),
         pltpu.VMEM(table.shape, BF16), pltpu.SemaphoreType.DMA((4,))],
    )(in_hbm(orders), in_hbm(lengths), in_hbm(x), in_hbm(table))


def slope_kernel(x_ref, low_ref, high_ref, lens_ref, weight_ref, rows_ref, table_ref, out_ref,
                 buffer, sem):
    held = []
    count = x_ref.shape[0] // 3
    for field in range(3):
        rows = pl.ds(field * count, count)
        stacked = jnp.concatenate([x_ref[rows, :], low_ref[rows, :], high_ref[rows, :]], axis=0)
        slope = dot(rows_ref[...], stacked, ((1,), (0,)))
        held.append(masked_rows(slope, lens_ref[...], weight_ref[...]))
    send_bands(table_ref, jnp.concatenate(held, axis=0), out_ref, buffer, sem)


def radial_slope(x, low, high, lens, weight, rows_map, table):
    rows = x.shape[0]
    return call(
        slope_kernel, "radial_slope", pltpu.HBM((R, rows), BF16), [HERE] * 7, FAR,
        [pltpu.VMEM((R, rows), BF16), pltpu.SemaphoreType.DMA((4,))],
    )(x, low, high, lens, weight, rows_map, table)


def sine_cosine(phase, points):
    centred = ((phase + points // 2) & (points - 1)) - points // 2
    y = centred.astype(F32) * (math.pi / points)
    square = y * y
    sine = jnp.float32(0.0)
    for n in (11, 9, 7, 5, 3, 1):
        sine = sine * square + (-1.0) ** (n // 2) / math.factorial(n)
    sine = sine * y
    cosine = jnp.float32(0.0)
    for n in (12, 10, 8, 6, 4, 2, 0):
        cosine = cosine * square + (-1.0) ** (n // 2) / math.factorial(n)
    return 1.0 - 2.0 * sine * sine, 2.0 * sine * cosine


def table_kernel(slots, orders_ref, far_ref, out_ref, sem):
    half = 128 * orders_ref.shape[0]
    points = 2 * half
    lane = lax.broadcasted_iota(jnp.int32, (slots, 128), 1)
    copies = []
    for row in range(orders_ref.shape[0]):
        column = jnp.broadcast_to(orders_ref[row:row + 1, :], (128, 128)).T
        for piece in range(128 // slots):
            orders = column[piece * slots:(piece + 1) * slots]
            rows = pl.ds(row * 128 + piece * slots, slots)
            cos_now, sin_now = sine_cosine((orders * lane) & (points - 1), points)
            cos_turn, sin_turn = sine_cosine((orders * 128) & (points - 1), points)
            for block in range(half // 128):
                out_ref[rows, pl.ds(block * 128, 128)] = cos_now.astype(BF16)
                out_ref[rows, pl.ds(half + (block + 1) * 128, 128)] = (-sin_now).astype(BF16)
                cos_now, sin_now = (
                    cos_now * cos_turn - sin_now * sin_turn,
                    sin_now * cos_turn + cos_now * sin_turn,
                )
            sign = jnp.where(lane == 0, 1 - 2 * (orders & 1), 0)
            out_ref[rows, pl.ds(half, 128)] = sign.astype(F32).astype(BF16)
        part = pl.ds(row * 128, 128)
        copies.append(pltpu.make_async_copy(out_ref.at[part], far_ref.at[part], sem.at[row]))
        copies[-1].start()
    for copy in copies:
        copy.wait()


def azimuthal_table(orders, slots):
    shape = (orders.size, 2 * orders.size + 128)
    return call(
        functools.partial(table_kernel, slots), "azimuthal_table",
        pltpu.HBM(shape, BF16), [HERE], FAR,
        [pltpu.VMEM(shape, BF16), pltpu.SemaphoreType.DMA((orders.shape[0],))],
    )(orders)


def place_field(lhs, row, bands, perm_ref, groups, band):
    per = perm_ref.shape[0] // bands.shape[1]
    stacked = jnp.concatenate([
        jnp.concatenate(
            [bands[(tile * per + e) * band:(tile * per + e + 1) * band] for e in range(per)], axis=1
        )
        for tile in range(groups // per)
    ], axis=0)
    mapped = dot(stacked, perm_ref[...], ((1,), (0,))).astype(BF16)
    for tile in range(groups // per):
        for plane in range(2):
            for part in range(2):
                lanes = (2 * plane + part) * 128
                lhs[part, row + plane * band:row + (plane + 1) * band,
                    pl.ds(tile * 128, 128)] = mapped[tile * band:(tile + 1) * band,
                                                     lanes:lanes + 128]


def table_loads(far_ref, table_ref, sem):
    rows, columns = table_ref.shape
    half = rows
    step = half // 2
    pieces = [(0, step), (half + 128, step), (step, step + 128), (half + 128 + step, step)]
    loads = []
    for start, size in pieces:
        loads.append([])
        for piece in range(4):
            area = (pl.ds(piece * (rows // 4), rows // 4), pl.ds(start, size))
            index = 4 * (len(loads) - 1) + piece
            loads[-1].append(pltpu.make_async_copy(
                far_ref.at[area], table_ref.at[area], sem.at[index]))
            loads[-1][-1].start()
    return pieces, loads


def axial_kernel(groups, band, raw_ref, perm_ref, far_ref, axial_ref, lhs, table_ref, sem):
    pieces, loads = table_loads(far_ref, table_ref, sem)
    place_field(lhs, 0, raw_ref[...], perm_ref, groups, band)
    half = table_ref.shape[0]
    for index, (start, size) in enumerate(pieces):
        for load in loads[index]:
            load.wait()
        part = pl.ds(start, size)
        values = dot(lhs[index % 2], table_ref[:, part], ((1,), (0,)))
        column = lax.broadcasted_iota(jnp.int32, values.shape, 1) + start
        once = (column == 0) | (column == half)
        axial_ref[:, part] = values * jnp.where(once, 1.0 / 12.0, 1.0 / 6.0)


def axial_stage(raw, perm, table, groups, band):
    rows, columns = table.shape
    return call(
        functools.partial(axial_kernel, groups, band), "axial_stage",
        jax.ShapeDtypeStruct((2 * band, columns), F32),
        [HERE, HERE, FAR], HERE,
        [pltpu.VMEM((2, 2 * band, rows), BF16), pltpu.VMEM(table.shape, BF16),
         pltpu.SemaphoreType.DMA((16,))],
    )(raw, perm, in_hbm(table))


def physical_kernel(groups, band, step, scale, slope_ref, axial_ref, perm_ref, far_ref, out_ref,
                    lhs, even, odd, table_ref, sem):
    pieces, loads = table_loads(far_ref, table_ref, sem)
    width = slope_ref.shape[1] // 3
    half = table_ref.shape[0]
    per = perm_ref.shape[0] // width
    for field in range(3):
        place_field(lhs, 2 * field * band, slope_ref[:, field * width:(field + 1) * width],
                    perm_ref, groups, band)
    for index in (0, 2):
        (start, size), (other, span) = pieces[index], pieces[index + 1]
        for load in loads[index]:
            load.wait()
        cosines = dot(lhs[0], table_ref[:, pl.ds(start, size)], ((1,), (0,)))
        for load in loads[index + 1]:
            load.wait()
        sines = dot(lhs[1], table_ref[:, pl.ds(other, span)], ((1,), (0,)))
        axial_cos = axial_ref[:, pl.ds(start, size)]
        axial_sin = axial_ref[:, pl.ds(other, span)]
        for g in range(3):
            area = slice(2 * g * band, (2 * g + 2) * band)
            c, s = cosines[area], sines[area]
            part = pl.ds(start, span)
            even[area, part] = (c[:, :span] * axial_cos[:, :span] + s * axial_sin).astype(BF16)
            odd[area, part] = (c[:, :span] * axial_sin + s * axial_cos[:, :span]).astype(BF16)
            if size > span:
                edge = (c[:, span:] * axial_cos[:, span:]).astype(BF16)
                even[area, pl.ds(start + span, size - span)] = edge

    for start in range(0, half, step):
        rows = pl.ds(start, step)
        parts = [
            (dot(even[...], table_ref[rows, 0:half + 128], ((1,), (1,))) * scale).astype(BF16),
            (dot(odd[...], table_ref[rows, half + 128:], ((1,), (1,))) * scale).astype(BF16),
        ]
        stacked = jnp.concatenate([
            jnp.concatenate([
                parts[part][(2 * g + plane) * band:(2 * g + plane + 1) * band,
                            tile * 128:(tile + 1) * 128]
                for plane in range(2) for part in range(2)
            ], axis=1)
            for g in range(3) for tile in range(step // 128)
        ], axis=0)
        mapped = dot(stacked, perm_ref[...], ((1,), (1,))).astype(BF16)
        for g in range(3):
            for tile in range(step // 128):
                source = (g * (step // 128) + tile) * band
                for e in range(per):
                    row = ((start // 128 + tile) * per + e) * band
                    out_ref[row:row + band, pl.ds(g * width, width)] = mapped[
                        source:source + band, e * width:(e + 1) * width]


def physical_stage(slope, axial, perm, table, groups, band, step=512):
    rows = table.shape[0]
    scale = math.sqrt(1.0 / rows)
    return call(
        functools.partial(physical_kernel, groups, band, step, scale), "physical_stage",
        jax.ShapeDtypeStruct(slope.shape, BF16), [HERE] * 3 + [FAR], HERE,
        [pltpu.VMEM((2, 6 * band, rows), BF16), pltpu.VMEM((6 * band, rows + 128), BF16),
         pltpu.VMEM((6 * band, rows), BF16), pltpu.VMEM(table.shape, BF16),
         pltpu.SemaphoreType.DMA((16,))],
        limit=28,
    )(slope, axial, perm, in_hbm(table))


def final_kernel(x_ref, lens_ref, table_ref, out_ref, buffer, sem):
    width = x_ref.shape[1] // 3
    modes = lax.broadcasted_iota(jnp.int32, (width, table_ref.shape[1]), 1)
    keep = modes < lens_ref[:, :1]
    copies = []
    for g in range(3):
        part = x_ref[:, g * width:(g + 1) * width]
        result = dot(part, table_ref[...], ((0,), (0,)))
        rows = jnp.where(keep, result, 0.0).astype(BF16)
        buffer[g] = rows.reshape(buffer.shape[1:])
        copies.append(pltpu.make_async_copy(buffer.at[g], out_ref.at[g], sem.at[g]))
        copies[-1].start()
    for copy in copies:
        copy.wait()


def radial_analysis(x, lens, table, shape):
    return call(
        final_kernel, "radial_analysis", pltpu.HBM(shape, BF16), [HERE] * 3, FAR,
        [pltpu.VMEM(shape, BF16), pltpu.SemaphoreType.DMA((3,))],
    )(x, lens, table)


def shift(block, offset):
    count = lax.axis_size("axial")
    return lax.ppermute(block, "axial", [(i, (i + offset) % count) for i in range(count)])


def exchange(block):
    return lax.all_to_all(block, "order", split_axis=0, concat_axis=0, tiled=True)


def shards(coefficients, order_lists, lengths):
    field_count, part_count, slots, planes, modes = coefficients.shape
    order_count = order_lists.shape[0]
    groups = lax.axis_size("order")
    band = R // groups
    width = part_count * slots * planes
    synthesis, analysis = radial_constants(R, modes)
    rows_map, perm = plane_matrices(slots)

    sloped = stage(coefficients)
    low, high = shift(sloped, 1), shift(sloped, -1)
    orders = order_lists.reshape(order_count // 128, 128)
    bands, lens, weight = radial_raw(
        orders, lengths.reshape(order_count // 128, 128), coefficients, synthesis
    )
    raw_bands = exchange(bands)
    table = azimuthal_table(orders, slots)
    raw_bands, later_synthesis = lax.optimization_barrier((raw_bands, jnp.asarray(synthesis)))
    slope_bands = exchange(
        radial_slope(sloped, low, high, lens, weight, rows_map, later_synthesis)
    )
    axial = axial_stage(raw_bands, perm, table, groups, band)
    spectral = physical_stage(slope_bands, axial, perm, table, groups, band)
    shape = (3, part_count, slots, planes, modes)
    return radial_analysis(exchange(spectral), lens, analysis, shape)


def solution(mesh):
    placed = (P(None, None, "order", "axial", None), P(), P())
    return jax.shard_map(
        shards,
        mesh=mesh,
        in_specs=placed,
        out_specs=P(None, None, "order", "axial", None),
        check_vma=False,
    )
```

```python
import functools
import math

import jax
import jax.numpy as jnp
import numpy as np
from jax import lax
from jax.experimental import pallas as pl
from jax.experimental.pallas import tpu as pltpu
from jax.sharding import PartitionSpec as P

R = 1024
F32 = jnp.float32
BF16 = jnp.bfloat16


def radial_constants(radius_count, mode_count):
    radius_ids = np.arange(radius_count)
    mode_ids = np.arange(mode_count)
    phases = mode_ids[None, :] * (2 * radius_ids[:, None] + 1) % (4 * radius_count)
    cosines = np.cos(phases * (math.pi / (2 * radius_count))).astype(np.float32)
    synthesis = cosines.astype(jnp.bfloat16)
    analysis = (cosines * np.float32(math.sqrt(2.0 / radius_count))).astype(jnp.bfloat16)
    return synthesis, analysis


def plane_matrices(slots):
    width = 2 * slots * 2
    eye = np.eye(width // 2, dtype=np.float32)
    own = np.kron(eye, np.array([[0, 8], [-8, 0]], np.float32))
    low = np.kron(eye, np.array([[1, -8], [0, 1]], np.float32))
    high = np.kron(eye, np.array([[-1, 0], [8, -1]], np.float32))
    rows = np.concatenate([own, low, high], axis=1)
    per = 128 // slots
    source = np.arange(per * width).reshape(per, 2, slots, 2).transpose(3, 1, 0, 2).reshape(-1)
    permutation = np.zeros((per * width, per * width), np.float32)
    permutation[source, np.arange(per * width)] = 1.0
    return rows.astype(jnp.bfloat16), permutation.astype(jnp.bfloat16)


def dot(a, b, dims):
    return lax.dot_general(a, b, (dims, ((), ())), preferred_element_type=F32)


HERE = pl.BlockSpec(memory_space=pltpu.VMEM)
FAR = pl.BlockSpec(memory_space=pltpu.HBM)
SCALARS = pl.BlockSpec(memory_space=pltpu.SMEM)


def in_hbm(x):
    return pltpu.with_memory_space_constraint(x, pltpu.HBM)


def call(kernel, name, out_shape, in_specs, out_specs, scratch=(), limit=16):
    return pl.pallas_call(
        kernel,
        out_shape=out_shape,
        in_specs=in_specs,
        out_specs=out_specs,
        scratch_shapes=list(scratch),
        compiler_params=pltpu.CompilerParams(vmem_limit_bytes=limit << 20),
        name=name,
    )


def stage_kernel(x_ref, out_ref, held, sem):
    fields, parts, slots = held.shape[:3]
    copies = []
    for field in range(fields):
        for part in range(parts):
            for half in range(2):
                area = (field, part, pl.ds(half * (slots // 2), slots // 2))
                copies.append(pltpu.make_async_copy(
                    x_ref.at[area], held.at[area], sem.at[len(copies)]))
                copies[-1].start()
    rows = out_ref.shape[0] // fields
    for field in range(fields):
        for copy in copies[4 * field:4 * field + 4]:
            copy.wait()
        out_ref[field * rows:(field + 1) * rows, :] = held[field].reshape(rows, held.shape[-1])


def stage(x):
    rows, modes = 3 * math.prod(x.shape[1:-1]), x.shape[-1]
    return call(
        stage_kernel, "stage", pltpu.VMEM((rows, modes), BF16),
        [FAR], HERE, [pltpu.VMEM((3,) + x.shape[1:], BF16), pltpu.SemaphoreType.DMA((12,))],
    )(in_hbm(x))


def masked_rows(block, lens, weight):
    modes = lax.broadcasted_iota(jnp.int32, block.shape, 1)
    return jnp.where(modes < lens[:, :1], block.astype(F32) * weight[:, :1], 0.0).astype(BF16)


def send_bands(table_ref, rows, out_ref, buffer, sem, loads=None, count=4):
    size = table_ref.shape[0] // count
    copies = []
    for i in range(count):
        part = pl.ds(i * size, size)
        if loads is not None:
            loads[i].wait()
        buffer[part, :] = dot(table_ref[part, :], rows, ((1,), (1,))).astype(BF16)
        copies.append(pltpu.make_async_copy(buffer.at[part], out_ref.at[part], sem.at[i]))
        copies[-1].start()
    for copy in copies:
        copy.wait()


def slot_rows(orders, lengths, slots):
    index = lax.axis_index("order")
    per_row = 128 // slots
    lane = lax.broadcasted_iota(jnp.int32, (128, 128), 1)
    held = jnp.broadcast_to(orders[pl.ds(index // per_row, 1), :], (128, 128)).T
    total = jnp.zeros((128, 128), F32)
    for row in range(lengths.shape[0]):
        wide = jnp.broadcast_to(lengths[row:row + 1, :], (128, 128)).astype(F32)
        total += jnp.where(held == lane + row * 128, wide, 0.0)
    found = jnp.sum(total, axis=1, keepdims=True).astype(jnp.int32)
    found = jnp.broadcast_to(found, (128, 128))
    zero = jnp.where(held == 0, 1, 0)
    columns = jnp.where(lane == 0, found >> 3, jnp.where(lane == 1, found & 7, zero))
    rows = lax.broadcasted_iota(jnp.int32, (2 * slots, 128), 0) // 2
    picked = lax.broadcasted_iota(jnp.int32, (2 * slots, 128), 1)
    pick = jnp.where(picked == rows + (index % per_row) * slots, 1.0, 0.0).astype(BF16)
    result = dot(pick, columns.astype(F32).astype(BF16), ((1,), (0,)))
    lens = (result[:, 0:1] * 8.0 + result[:, 1:2]).astype(jnp.int32)
    weight = 2.0 - result[:, 2:3]
    return jnp.concatenate([lens, lens], axis=0), jnp.concatenate([weight, weight], axis=0)


def raw_kernel(orders_far, lengths_far, x_far, table, out_ref, lens_ref, weight_ref,
               buffer, sem, orders, lengths, x_ref, small_sem):
    small = [
        pltpu.make_async_copy(orders_far, orders, small_sem.at[0]),
        pltpu.make_async_copy(lengths_far, lengths, small_sem.at[1]),
        pltpu.make_async_copy(x_far.at[3, 0], x_ref.at[0], small_sem.at[2]),
        pltpu.make_async_copy(x_far.at[3, 1], x_ref.at[1], small_sem.at[3]),
    ]
    for copy in small:
        copy.start()
    small[0].wait()
    small[1].wait()
    lens, weight = slot_rows(orders, lengths, x_ref.shape[1])
    lens_ref[...] = jnp.broadcast_to(lens, lens_ref.shape)
    weight_ref[...] = jnp.broadcast_to(weight, weight_ref.shape)
    small[2].wait()
    small[3].wait()
    block = x_ref[...]
    block = block.reshape(math.prod(block.shape[:-1]), block.shape[-1])
    send_bands(table, masked_rows(block, lens, weight), out_ref, buffer, sem)


def radial_raw(orders, lengths, x, table):
    rows = math.prod(x.shape[1:-1])
    return call(
        raw_kernel, "radial_raw",
        (pltpu.HBM((R, rows), BF16),
         jax.ShapeDtypeStruct((rows, 128), jnp.int32),
         jax.ShapeDtypeStruct((rows, 128), F32)),
        [FAR] * 3 + [HERE], (FAR, HERE, HERE),
        [pltpu.VMEM((R, rows), BF16), pltpu.SemaphoreType.DMA((4,)),
         pltpu.VMEM(orders.shape, jnp.int32), pltpu.VMEM(lengths.shape, jnp.int32),
         pltpu.VMEM(x.shape[1:], BF16), pltpu.SemaphoreType.DMA((4,))],
    )(in_hbm(orders), in_hbm(lengths), in_hbm(x), table)


def slope_kernel(x_ref, low_ref, high_ref, lens_ref, weight_ref, rows_ref, table_ref, out_ref,
                 buffer, sem):
    held = []
    count = x_ref.shape[0] // 3
    for field in range(3):
        rows = pl.ds(field * count, count)
        stacked = jnp.concatenate([x_ref[rows, :], low_ref[rows, :], high_ref[rows, :]], axis=0)
        slope = dot(rows_ref[...], stacked, ((1,), (0,)))
        held.append(masked_rows(slope, lens_ref[...], weight_ref[...]))
    send_bands(table_ref, jnp.concatenate(held, axis=0), out_ref, buffer, sem)


def radial_slope(x, low, high, lens, weight, rows_map, table):
    rows = x.shape[0]
    return call(
        slope_kernel, "radial_slope", pltpu.HBM((R, rows), BF16), [HERE] * 7, FAR,
        [pltpu.VMEM((R, rows), BF16), pltpu.SemaphoreType.DMA((4,))],
    )(x, low, high, lens, weight, rows_map, table)


def sine_cosine(phase, points):
    centred = ((phase + points // 2) & (points - 1)) - points // 2
    y = centred.astype(F32) * (math.pi / points)
    square = y * y
    sine = jnp.float32(0.0)
    for n in (11, 9, 7, 5, 3, 1):
        sine = sine * square + (-1.0) ** (n // 2) / math.factorial(n)
    sine = sine * y
    cosine = jnp.float32(0.0)
    for n in (12, 10, 8, 6, 4, 2, 0):
        cosine = cosine * square + (-1.0) ** (n // 2) / math.factorial(n)
    return 1.0 - 2.0 * sine * sine, 2.0 * sine * cosine


def table_kernel(slots, orders_ref, far_ref, out_ref, sem):
    half = 128 * orders_ref.shape[0]
    points = 2 * half
    lane = lax.broadcasted_iota(jnp.int32, (slots, 128), 1)
    copies = []
    for row in range(orders_ref.shape[0]):
        column = jnp.broadcast_to(orders_ref[row:row + 1, :], (128, 128)).T
        for piece in range(128 // slots):
            orders = column[piece * slots:(piece + 1) * slots]
            rows = pl.ds(row * 128 + piece * slots, slots)
            cos_now, sin_now = sine_cosine((orders * lane) & (points - 1), points)
            cos_turn, sin_turn = sine_cosine((orders * 128) & (points - 1), points)
            for block in range(half // 128):
                out_ref[rows, pl.ds(block * 128, 128)] = cos_now.astype(BF16)
                out_ref[rows, pl.ds(half + (block + 1) * 128, 128)] = (-sin_now).astype(BF16)
                cos_now, sin_now = (
                    cos_now * cos_turn - sin_now * sin_turn,
                    sin_now * cos_turn + cos_now * sin_turn,
                )
            sign = jnp.where(lane == 0, 1 - 2 * (orders & 1), 0)
            out_ref[rows, pl.ds(half, 128)] = sign.astype(F32).astype(BF16)
        part = pl.ds(row * 128, 128)
        copies.append(pltpu.make_async_copy(out_ref.at[part], far_ref.at[part], sem.at[row]))
        copies[-1].start()
    for copy in copies:
        copy.wait()


def azimuthal_table(orders, slots):
    shape = (orders.size, 2 * orders.size + 128)
    return call(
        functools.partial(table_kernel, slots), "azimuthal_table",
        pltpu.HBM(shape, BF16), [HERE], FAR,
        [pltpu.VMEM(shape, BF16), pltpu.SemaphoreType.DMA((orders.shape[0],))],
    )(orders)


def place_field(lhs, row, bands, perm_ref, groups, band):
    per = perm_ref.shape[0] // bands.shape[1]
    stacked = jnp.concatenate([
        jnp.concatenate(
            [bands[(tile * per + e) * band:(tile * per + e + 1) * band] for e in range(per)], axis=1
        )
        for tile in range(groups // per)
    ], axis=0)
    mapped = dot(stacked, perm_ref[...], ((1,), (0,))).astype(BF16)
    for tile in range(groups // per):
        for plane in range(2):
            for part in range(2):
                lanes = (2 * plane + part) * 128
                lhs[part, row + plane * band:row + (plane + 1) * band,
                    pl.ds(tile * 128, 128)] = mapped[tile * band:(tile + 1) * band,
                                                     lanes:lanes + 128]


def table_loads(far_ref, table_ref, sem):
    rows, columns = table_ref.shape
    half = rows
    step = half // 2
    pieces = [(0, step), (half + 128, step), (step, step + 128), (half + 128 + step, step)]
    loads = []
    for start, size in pieces:
        loads.append([])
        for piece in range(4):
            area = (pl.ds(piece * (rows // 4), rows // 4), pl.ds(start, size))
            index = 4 * (len(loads) - 1) + piece
            loads[-1].append(pltpu.make_async_copy(
                far_ref.at[area], table_ref.at[area], sem.at[index]))
            loads[-1][-1].start()
    return pieces, loads


def axial_kernel(groups, band, raw_ref, perm_ref, far_ref, axial_ref, lhs, table_ref, sem):
    pieces, loads = table_loads(far_ref, table_ref, sem)
    place_field(lhs, 0, raw_ref[...], perm_ref, groups, band)
    half = table_ref.shape[0]
    for index, (start, size) in enumerate(pieces):
        for load in loads[index]:
            load.wait()
        part = pl.ds(start, size)
        values = dot(lhs[index % 2], table_ref[:, part], ((1,), (0,)))
        column = lax.broadcasted_iota(jnp.int32, values.shape, 1) + start
        once = (column == 0) | (column == half)
        axial_ref[:, part] = values * jnp.where(once, 1.0 / 12.0, 1.0 / 6.0)


def axial_stage(raw, perm, table, groups, band):
    rows, columns = table.shape
    return call(
        functools.partial(axial_kernel, groups, band), "axial_stage",
        jax.ShapeDtypeStruct((2 * band, columns), F32),
        [HERE, HERE, FAR], HERE,
        [pltpu.VMEM((2, 2 * band, rows), BF16), pltpu.VMEM(table.shape, BF16),
         pltpu.SemaphoreType.DMA((16,))],
    )(raw, perm, in_hbm(table))


def physical_kernel(groups, band, step, scale, slope_ref, axial_ref, perm_ref, far_ref, out_ref,
                    lhs, even, odd, table_ref, sem):
    pieces, loads = table_loads(far_ref, table_ref, sem)
    width = slope_ref.shape[1] // 3
    half = table_ref.shape[0]
    per = perm_ref.shape[0] // width
    for field in range(3):
        place_field(lhs, 2 * field * band, slope_ref[:, field * width:(field + 1) * width],
                    perm_ref, groups, band)
    for index in (0, 2):
        (start, size), (other, span) = pieces[index], pieces[index + 1]
        for load in loads[index]:
            load.wait()
        cosines = dot(lhs[0], table_ref[:, pl.ds(start, size)], ((1,), (0,)))
        for load in loads[index + 1]:
            load.wait()
        sines = dot(lhs[1], table_ref[:, pl.ds(other, span)], ((1,), (0,)))
        axial_cos = axial_ref[:, pl.ds(start, size)]
        axial_sin = axial_ref[:, pl.ds(other, span)]
        for g in range(3):
            area = slice(2 * g * band, (2 * g + 2) * band)
            c, s = cosines[area], sines[area]
            part = pl.ds(start, span)
            even[area, part] = (c[:, :span] * axial_cos[:, :span] + s * axial_sin).astype(BF16)
            odd[area, part] = (c[:, :span] * axial_sin + s * axial_cos[:, :span]).astype(BF16)
            if size > span:
                edge = (c[:, span:] * axial_cos[:, span:]).astype(BF16)
                even[area, pl.ds(start + span, size - span)] = edge

    for start in range(0, half, step):
        rows = pl.ds(start, step)
        parts = [
            (dot(even[...], table_ref[rows, 0:half + 128], ((1,), (1,))) * scale).astype(BF16),
            (dot(odd[...], table_ref[rows, half + 128:], ((1,), (1,))) * scale).astype(BF16),
        ]
        stacked = jnp.concatenate([
            jnp.concatenate([
                parts[part][(2 * g + plane) * band:(2 * g + plane + 1) * band,
                            tile * 128:(tile + 1) * 128]
                for plane in range(2) for part in range(2)
            ], axis=1)
            for g in range(3) for tile in range(step // 128)
        ], axis=0)
        mapped = dot(stacked, perm_ref[...], ((1,), (1,))).astype(BF16)
        for g in range(3):
            for tile in range(step // 128):
                source = (g * (step // 128) + tile) * band
                for e in range(per):
                    row = ((start // 128 + tile) * per + e) * band
                    out_ref[row:row + band, pl.ds(g * width, width)] = mapped[
                        source:source + band, e * width:(e + 1) * width]


def physical_stage(slope, axial, perm, table, groups, band, step=512):
    rows = table.shape[0]
    scale = math.sqrt(1.0 / rows)
    return call(
        functools.partial(physical_kernel, groups, band, step, scale), "physical_stage",
        jax.ShapeDtypeStruct(slope.shape, BF16), [HERE] * 3 + [FAR], HERE,
        [pltpu.VMEM((2, 6 * band, rows), BF16), pltpu.VMEM((6 * band, rows + 128), BF16),
         pltpu.VMEM((6 * band, rows), BF16), pltpu.VMEM(table.shape, BF16),
         pltpu.SemaphoreType.DMA((16,))],
        limit=28,
    )(slope, axial, perm, in_hbm(table))


def final_kernel(x_ref, lens_ref, table_ref, out_ref, buffer, sem):
    width = x_ref.shape[1] // 3
    modes = lax.broadcasted_iota(jnp.int32, (width, table_ref.shape[1]), 1)
    keep = modes < lens_ref[:, :1]
    copies = []
    for g in range(3):
        part = x_ref[:, g * width:(g + 1) * width]
        result = dot(part, table_ref[...], ((0,), (0,)))
        rows = jnp.where(keep, result, 0.0).astype(BF16)
        buffer[g] = rows.reshape(buffer.shape[1:])
        copies.append(pltpu.make_async_copy(buffer.at[g], out_ref.at[g], sem.at[g]))
        copies[-1].start()
    for copy in copies:
        copy.wait()


def radial_analysis(x, lens, table, shape):
    return call(
        final_kernel, "radial_analysis", pltpu.HBM(shape, BF16), [HERE] * 3, FAR,
        [pltpu.VMEM(shape, BF16), pltpu.SemaphoreType.DMA((3,))],
    )(x, lens, table)


def shift(block, offset):
    count = lax.axis_size("axial")
    return lax.ppermute(block, "axial", [(i, (i + offset) % count) for i in range(count)])


def exchange(block):
    return lax.all_to_all(block, "order", split_axis=0, concat_axis=0, tiled=True)


def shards(coefficients, order_lists, lengths):
    field_count, part_count, slots, planes, modes = coefficients.shape
    order_count = order_lists.shape[0]
    groups = lax.axis_size("order")
    band = R // groups
    width = part_count * slots * planes
    synthesis, analysis = radial_constants(R, modes)
    rows_map, perm = plane_matrices(slots)

    sloped = stage(coefficients)
    low, high = shift(sloped, 1), shift(sloped, -1)
    orders = order_lists.reshape(order_count // 128, 128)
    bands, lens, weight = radial_raw(
        orders, lengths.reshape(order_count // 128, 128), coefficients, synthesis
    )
    raw_bands = exchange(bands)
    table = azimuthal_table(orders, slots)
    raw_bands, later_synthesis = lax.optimization_barrier((raw_bands, jnp.asarray(synthesis)))
    slope_bands = exchange(
        radial_slope(sloped, low, high, lens, weight, rows_map, later_synthesis)
    )
    axial = axial_stage(raw_bands, perm, table, groups, band)
    spectral = physical_stage(slope_bands, axial, perm, table, groups, band)
    shape = (3, part_count, slots, planes, modes)
    return radial_analysis(exchange(spectral), lens, analysis, shape)


def solution(mesh):
    placed = (P(None, None, "order", "axial", None), P(), P())
    return jax.shard_map(
        shards,
        mesh=mesh,
        in_specs=placed,
        out_specs=P(None, None, "order", "axial", None),
        check_vma=False,
    )
```
